32 devices in a mesh: grp: 2 (over core), blk: 16 (over z, y, x).
Axes of the slice: x: 2, y: 2, z: 4, core: 2. Of those that a mesh axis runs over, the one named last changes fastest.
Arguments:
- ints: bfloat16 [16, 1536, 4096], P('blk', 'grp'), may hold values from -0.375 to 0.375
- occ_energy: float32 [400], replicated, may hold values from -2 to -0.3
- occ_window: int32 [16], replicated, may hold values from 0 to 399, as said below
- virt_energy: float32 [1536], replicated, may hold values from 0.3 to 3
Outputs:
- virt_density: float32 [1536, 768], P(('grp', 'blk'))
- pair_energy: float32 [16, 4], P('blk')
The draws below stay inside these ranges and needn't reach their ends.
Inputs may be any that keep to these rules, and one draw needn't show every extreme that they name: `occ_window`: distinct indices into occ_energy.
All inputs are finite; a program needn't handle non-finite values.
Results may differ from the reference program's by a relative error of at most 0.0003.
Values may be sent and summed in bfloat16 or wider, within the bound.
A program may use at most 64 MiB of HBM per device.

```python
import jax
import jax.numpy as jnp
from jax import lax

NVIRT = 1536
NAUX = 4096
NOCC_ALL = 400
OCC_DEV = 1
STEPS = 4
NOCC = 16
N_GRP = 2
N_BLK = 16


def draw_occ_window(key, part):
    return jax.random.permutation(key, NOCC_ALL)[:NOCC].astype(jnp.int32)


def spiked(array, rng, source, target, parts, factor):
    owner, partner = [(jnp.arange(array.shape[axis_at]) // (array.shape[axis_at] // parts)).reshape([-1 if axis == axis_at else 1 for axis in range(array.ndim)]) for axis_at in (source, target)]
    chosen = jax.random.permutation(rng, parts)[partner]
    strong = (owner == chosen) | (owner == (partner + parts // 2) % parts)
    return jnp.where(strong, factor * array, array)


def steps_of(stream_key, dims, split, least, largest):
    gain, own = 1.0, jax.random.fold_in(stream_key, 6)
    for position, shards_of in split:
        steps = jnp.exp(jax.random.uniform(jax.random.fold_in(own, position), (shards_of,), jnp.float32, least / len(split), largest / len(split)))
        gain = gain * jnp.repeat(steps, dims[position] // shards_of).reshape([-1 if axis == position else 1 for axis in range(len(dims))])
    return gain


def bell_draw_with(stream_key, dims, scale, reach, shards, heavy, kind=jnp.bfloat16):
    drawn = scale * jax.random.normal(stream_key, dims, jnp.float32)
    if shards:
        drawn = drawn * steps_of(stream_key, dims, shards, -0.22, 0.18)
    return jnp.clip(spiked(drawn, jax.random.fold_in(stream_key, 3), *heavy), -reach, reach).astype(kind)


def setup_inputs(seed: int = 0) -> dict:
    keys = jax.random.split(jax.random.key(seed), 5)
    ints = bell_draw_with(keys[0], (NOCC, NVIRT, NAUX), (0.5 * NAUX ** -0.25), 0.375, ((0, 16), (1, 2)), (0, 1, 16, 2.0))
    occ_energy = jnp.clip(jax.random.uniform(keys[1], (NOCC_ALL,), jnp.float32, -2.0, -0.3), -2.0, -0.3)
    occ_window = draw_occ_window(jax.random.fold_in(keys[4], 71), 0)
    virt_energy = jnp.clip(jax.random.uniform(keys[3], (NVIRT,), jnp.float32, 0.3, 3.0), 0.3, 3.0)
    return {"ints": ints, "occ_energy": occ_energy, "occ_window": occ_window, "virt_energy": virt_energy}


def reference(ints, occ_energy, occ_window, virt_energy):
    occ_levels = occ_energy[occ_window]
    block_size = NVIRT // N_GRP
    pair_blocks = N_GRP // 2
    virt_pairs = virt_energy.reshape(pair_blocks, 2 * block_size)
    window_pos = jnp.arange(NOCC, dtype=jnp.int32)
    density = jnp.zeros((NVIRT, block_size), jnp.float32)
    energy_list = []
    for cycle_step in range(STEPS):
        for within in range(OCC_DEV):
            partner_idx = (((window_pos // OCC_DEV - cycle_step) % N_BLK) * OCC_DEV + within).astype(jnp.int32)
            occ_partner = occ_levels[partner_idx]

            def single_pair(inputs_in):
                row_ints, partner_at, occ_row, occ_col = inputs_in
                col_ints = lax.dynamic_index_in_dim(ints, partner_at, 0, keepdims=False)
                left = row_ints.astype(jnp.float32).reshape(pair_blocks, 2 * block_size, NAUX)
                right = col_ints.astype(jnp.float32).reshape(pair_blocks, 2 * block_size, NAUX)
                coupling = jnp.einsum('qap,qbp->qab', left, right, precision=lax.Precision.HIGHEST)
                denominator = virt_pairs[:, :, None] + virt_pairs[:, None, :] - occ_row - occ_col
                amplitude = coupling / denominator
                product = jnp.einsum('qab,qcb->qac', amplitude, amplitude, precision=lax.Precision.HIGHEST)
                blocks = jnp.stack([product[:, :block_size, :block_size], product[:, block_size:, block_size:]], 1)
                pair_value = -jnp.sum(amplitude * coupling) / (block_size * block_size)
                return blocks.reshape(NVIRT, block_size), pair_value

            blocks, values = lax.map(single_pair, (ints, partner_idx, occ_levels, occ_partner))
            density = density + jnp.sum(blocks, axis=0)
            energy_list.append(values)
    return density / (NOCC * STEPS * OCC_DEV), jnp.stack(energy_list, axis=1)
```

```python
import functools

import jax
import jax.numpy as jnp
from jax import lax
from jax.experimental import pallas as pl
from jax.experimental.pallas import tpu as pltpu
from jax.sharding import PartitionSpec as P

STEPS = 4
CHUNKS = 1
RELAY = False


def from_partner(block, axis, stride):
    count = lax.axis_size(axis)
    route = []
    for low in range(count):
        high = low | 1 << stride
        if high != low and high < count:
            route += [(low, high), (high, low)]
    return lax.ppermute(block, axis, route)


def shifted(shard, axis, by):
    peers = lax.axis_size(axis)
    return lax.ppermute(shard, axis, [(i, (i + by) % peers) for i in range(peers)])


def lookup_many(values_in, where_at):
    positions = jnp.arange(values_in.shape[0], dtype=jnp.int32)
    matches = positions[None, :] == where_at[:, None]
    return jnp.sum(
        jnp.where(matches, values_in[None, :], jnp.zeros_like(values_in)[None, :]), axis=1
    )


def fetched(pieces, block_index, block_count):
    if not RELAY or block_count % 4:
        return (
            [shifted(piece, "blk", -2) for piece in pieces],
            [shifted(piece, "blk", 1) for piece in pieces],
        )
    blocks = range(block_count)
    cross_y = [(c, c ^ 2) for c in blocks]
    down = [(c, (c - 4) % block_count) for c in blocks if c & 2]
    evens = [(c, c + 1) for c in blocks if c % 2 == 0]
    odds = [(c, (c + (-1 if c & 2 else 3)) % block_count) for c in blocks if c % 2]
    upper = (block_index & 2) != 0
    odd = (block_index & 1) != 0
    further, back = [], []
    for piece in pieces:
        over = lax.ppermute(piece, "blk", cross_y)
        direct = lax.ppermute(piece, "blk", evens)
        relayed = lax.ppermute(over, "blk", odds)
        further.append(jnp.where(upper, lax.ppermute(over, "blk", down), over))
        back.append(jnp.where(odd, direct, relayed))
    return further, back


def local(ints, occ_energy, occ_window, virt_energy):
    occ_dev = ints.shape[0]
    virt_width = ints.shape[1]
    occ_count = occ_window.shape[0]
    block_count = occ_count // occ_dev
    group_index = lax.axis_index("grp")
    block_index = lax.axis_index("blk")
    mirror_index = group_index + 1 - 2 * (group_index % 2)
    virt_own = lax.dynamic_slice_in_dim(virt_energy, group_index * virt_width, virt_width)
    virt_mirror = lax.dynamic_slice_in_dim(virt_energy, mirror_index * virt_width, virt_width)
    local_rows = jnp.arange(occ_dev, dtype=jnp.int32)

    def levels(offset):
        block = (block_index + offset) % block_count
        return lookup_many(occ_energy, lookup_many(occ_window, block * occ_dev + local_rows))

    occ_own, occ_back, occ_further = levels(0), levels(-1), levels(2)
    chunks = CHUNKS if virt_width % (16 * CHUNKS) == 0 else 1
    size = virt_width // chunks
    pieces = [ints[:, n * size : (n + 1) * size] for n in range(chunks)]
    mirror = from_partner(ints, "grp", 0)
    further_pieces, back_pieces = fetched(pieces, block_index, block_count)
    virt_pieces = [
        (virt_own[n * size : (n + 1) * size], virt_mirror[n * size : (n + 1) * size])
        for n in range(chunks)
    ]

    def tile(rows, cols, virt_cols, occ_rows, occ_cols):
        coupling = jnp.einsum("rap,tbp->rtab", rows, cols, preferred_element_type=jnp.float32)
        denominator = (
            virt_own[None, None, :, None]
            + virt_cols[None, None, None, :]
            - occ_rows[:, None, None, None]
            - occ_cols[None, :, None, None]
        )
        amplitude = coupling / denominator
        square = amplitude * amplitude
        energy = -jnp.sum(square * denominator, axis=(2, 3)) / (virt_width * virt_width)
        kept = lax.reduce_precision(amplitude, exponent_bits=8, mantissa_bits=7)
        high = kept.astype(jnp.bfloat16)
        low = (amplitude - kept).astype(jnp.bfloat16)
        main = jnp.einsum("rtab,rtcb->ac", high, high, preferred_element_type=jnp.float32)
        side = jnp.einsum("rtab,rtcb->ac", high, low, preferred_element_type=jnp.float32)
        return main, side, energy

    def add(one, other):
        return tuple(a + b for a, b in zip(one, other))

    zero = add(
        tile(ints, ints, virt_own, occ_own, occ_own),
        tile(ints, mirror, virt_mirror, occ_own, occ_own),
    )
    one = None
    for piece, (near, far) in zip(back_pieces, virt_pieces):
        part = add(
            tile(ints, piece, near, occ_own, occ_back),
            tile(ints, from_partner(piece, "grp", 0), far, occ_own, occ_back),
        )
        one = part if one is None else add(one, part)
    further = jnp.concatenate(further_pieces, axis=1)
    two = add(
        tile(further, ints, virt_own, occ_further, occ_own),
        tile(further, mirror, virt_mirror, occ_further, occ_own),
    )
    three = None
    for piece, (near, far) in zip(back_pieces, virt_pieces):
        part = add(
            tile(further, piece, near, occ_further, occ_back),
            tile(further, from_partner(piece, "grp", 0), far, occ_further, occ_back),
        )
        three = part if three is None else add(three, part)
    main, side = add(add(zero[:2], one[:2]), add(two[:2], three[:2]))
    density = main + side + side.T
    shares = lax.psum_scatter(density, "blk", scatter_dimension=0, tiled=True) / (
        occ_count * STEPS * occ_dev
    )
    sent = shifted(jnp.concatenate([two[2], three[2]], axis=1), "blk", 2)
    energies = jnp.concatenate([zero[2], one[2], sent], axis=1)
    return (shares, energies + from_partner(energies, "grp", 0))


MESH = pl.DeviceIdType.MESH
TILE = 256
SLICE = 256
ROWS = 64
NT = (((1,), (1,)), ((), ()))


def product(rows, cols):
    return lax.dot_general(rows, cols, NT, preferred_element_type=jnp.float32)


def fused_kernel(
    count,
    ints_ref,
    energy_ref,
    window_ref,
    virt_ref,
    density_ref,
    pairs_ref,
    buf,
    mir,
    acc,
    dens,
    split,
    rows_virt,
    cols_virt,
    first_in,
    second_in,
    third_in,
    evec,
    ein,
    etot,
    eback,
    efar,
    efin,
    load_sem,
    send_sem,
    recv_sem,
    mirror_send,
    mirror_recv,
    first_send,
    first_recv,
    second_send,
    second_recv,
    third_send,
    third_recv,
    energy_send,
    energy_recv,
):
    g = lax.axis_index("grp")
    me = lax.axis_index("blk")
    slices, width, depth = buf.shape[1:]
    layers = count // 4
    slab = dens.shape[3]
    tiles = width // TILE
    parts = width // 128
    place = me % 4
    x_at, y_at, z_at = me % 2, (me // 2) % 2, me // 4
    odd = place % 2
    even = odd == 0
    mirror = g + 1 - 2 * (g % 2)

    def at(offset):
        return (me + offset + count) % count

    x_peer = me + 1 - 2 * x_at
    y_peer = me + 2 - 4 * y_at
    is_two = (place // 2) * (1 - odd)
    col_to = at(1 - 2 * odd + 4 * (place // 3))
    other_to = at(2 - 4 * ((place + 3) // 4))
    other_slot = 2 + odd
    b_slot = 2 * (1 - odd)
    r_slot = 3 - 3 * is_two
    col_id = at(1 - 2 * ((place + 3) // 4) - 2 * is_two)
    b_id = at((1 - odd) * (2 - 4 * is_two))
    r_id = at(2 * odd + 4 * (1 - odd) * (1 - is_two))

    barrier = pltpu.get_barrier_semaphore()
    peers = [(g, x_peer), (mirror, me)]
    peers += [(g, at(o)) for o in (2, -2, 3, -3)]
    peers += [(g, at(4 * n)) for n in range(1, layers)]
    for peer in peers:
        pl.semaphore_signal(barrier, inc=1, device_id=peer, device_id_type=MESH)

    def load(k):
        return pltpu.make_async_copy(
            ints_ref.at[:, pl.ds(pl.multiple_of(k * depth, depth), depth)],
            buf.at[0, k],
            load_sem.at[k],
        )

    def flow(lane, k, slot, to):
        return pltpu.make_async_remote_copy(
            src_ref=buf.at[0, k],
            dst_ref=buf.at[slot, k],
            send_sem=send_sem.at[lane, k],
            recv_sem=recv_sem.at[lane, k],
            device_id=(g, to),
            device_id_type=MESH,
        )

    def flow_col(k):
        return flow(0, k, 1, col_to)

    def flow_other(k):
        return flow(1, k, other_slot, other_to)

    def flow_down(k):
        return flow(2, k, 3, at(-4))

    def reflect(slot, k):
        return pltpu.make_async_remote_copy(
            src_ref=buf.at[slot, k],
            dst_ref=mir.at[slot, k],
            send_sem=mirror_send.at[slot, k],
            recv_sem=mirror_recv.at[slot, k],
            device_id=(mirror, me),
            device_id_type=MESH,
        )

    @pl.loop(0, slices)
    def _(k):
        load(k).start()

    pl.semaphore_wait(barrier, len(peers))

    @pl.loop(0, slices)
    def _(k):
        load(k).wait()
        flow_col(k).start()
        flow_other(k).start()

        @pl.when(place == 0)
        def _():
            flow_down(k).start()

        reflect(0, k).start()

    def virt_row(group):
        return virt_ref[:, pl.ds(pl.multiple_of(group * width, 128), width)]

    mine, theirs = virt_row(g), virt_row(mirror)
    for n in range(tiles):
        cols_virt[n] = mine[:, n * TILE : (n + 1) * TILE]
        cols_virt[tiles + n] = theirs[:, n * TILE : (n + 1) * TILE]
    for n in range(width // 128):
        rows_virt[n * 128 : (n + 1) * 128, :] = jnp.transpose(
            jnp.broadcast_to(mine[:, n * 128 : (n + 1) * 128], (128, 128))
        )

    def level(index):
        return energy_ref[window_ref[index]]

    own_level, col_level, b_level, r_level = level(me), level(col_id), level(b_id), level(r_id)

    def clear(pair):
        @pl.loop(0, 2 * tiles)
        def _(n):
            acc[pair, n] = jnp.zeros(acc.shape[2:], jnp.float32)

    def couple_near(pair, row_slot, col_slot, k):
        rows = buf[row_slot, k]
        for n in range(tiles):
            acc[pair, n] += product(rows, buf[col_slot, k, n * TILE : (n + 1) * TILE, :])

    def couple_far(pair, row_slot, col_slot, k):
        rows = buf[row_slot, k]
        for n in range(tiles):
            acc[pair, tiles + n] += product(rows, mir[col_slot, k, n * TILE : (n + 1) * TILE, :])

    def amplitudes(pair, n, levels, energy_at, side):
        total = jnp.zeros((8, 128), jnp.float32)
        for r in range(width // ROWS):
            span = slice(r * ROWS, (r + 1) * ROWS)
            base = rows_virt[span, :] - levels
            for h in range(TILE // 128):
                lanes = slice(h * 128, (h + 1) * 128)
                coupling = acc[pair, n, span, lanes]
                amplitude = coupling / (base + cols_virt[n, :, lanes])
                term = amplitude * coupling
                total = total + jnp.sum(term.reshape(ROWS // 8, 8, 128), axis=0)
                high = amplitude.astype(jnp.bfloat16)
                split[side, 0, span, lanes] = high
                split[side, 1, span, lanes] = (amplitude - high.astype(jnp.float32)).astype(
                    jnp.bfloat16
                )
        evec[energy_at] += total

    def slabs_of(start, stop):
        for s in range(start // slab, -(-stop // slab)):
            low, high = max(start, s * slab), min(stop, (s + 1) * slab)
            yield (s // 4, (s // 2) % 2, s % 2), low, high, s * slab

    def densities(side):
        for n in range(tiles):
            start = n * TILE
            high, low = (split[side, h, start : start + TILE, :] for h in range(2))
            others_high, others_low = (split[side, h, start:, :] for h in range(2))
            update = product(
                jnp.concatenate([high, high, low], axis=1),
                jnp.concatenate([others_high, others_low, others_high], axis=1),
            )
            for where, low_row, high_row, origin in slabs_of(start, start + TILE):
                dens[(*where, slice(low_row - origin, high_row - origin), slice(start, None))] += (
                    update[low_row - start : high_row - start]
                )

    evec[...] = jnp.zeros(evec.shape, jnp.float32)
    dens[...] = jnp.zeros(dens.shape, jnp.float32)

    clear(0)

    @pl.loop(0, slices)
    def _(k):
        couple_near(0, 0, 0, k)

    @pl.loop(0, slices)
    def _(k):
        reflect(0, k).wait_recv()
        couple_far(0, 0, 0, k)

    amplitudes(0, 0, own_level + own_level, 0, 0)

    @pl.loop(1, 2 * tiles)
    def _(n):
        amplitudes(0, n, own_level + own_level, 0, n % 2)
        densities((n + 1) % 2)

    densities((2 * tiles - 1) % 2)

    for pair in range(3):
        clear(pair)

    @pl.loop(0, slices)
    def _(k):
        flow_col(k).wait_recv()
        reflect(1, k).start()
        flow_other(k).wait_recv()

        @pl.when(even)
        def _():
            reflect(2, k).start()

        @pl.when(place == 0)
        def _():
            flow_down(k).wait_recv()

        couple_near(0, b_slot, 1, k)
        couple_near(1, r_slot, b_slot, k)
        couple_near(2, r_slot, 1, k)
        reflect(1, k).wait_recv()

        @pl.when(even)
        def _():
            reflect(2, k).wait_recv()

        couple_far(0, b_slot, 1, k)
        couple_far(1, r_slot, b_slot, k)
        couple_far(2, r_slot, 1, k)

    def levels_of(pair):
        return jnp.where(
            pair == 0,
            b_level + col_level,
            jnp.where(pair == 1, r_level + b_level, r_level + col_level),
        )

    amplitudes(0, 0, levels_of(0), 1, 0)

    @pl.loop(1, 6 * tiles)
    def _(t):
        pair, n = t // (2 * tiles), t % (2 * tiles)
        amplitudes(pair, n, levels_of(pair), 1 + pair, t % 2)
        densities((t + 1) % 2)

    densities((6 * tiles - 1) % 2)

    for n in range(tiles):
        for m in range(n + 1, tiles):
            block = []
            for where, low_row, high_row, origin in slabs_of(n * TILE, (n + 1) * TILE):
                block.append(
                    dens[
                        (
                            *where,
                            slice(low_row - origin, high_row - origin),
                            slice(m * TILE, (m + 1) * TILE),
                        )
                    ]
                )
            turned = jnp.transpose(jnp.concatenate(block, axis=0))
            for where, low_row, high_row, origin in slabs_of(m * TILE, (m + 1) * TILE):
                dens[
                    (
                        *where,
                        slice(low_row - origin, high_row - origin),
                        slice(n * TILE, (n + 1) * TILE),
                    )
                ] = turned[low_row - m * TILE : high_row - m * TILE]

    def remote(source, target, sent, received, to):
        return pltpu.make_async_remote_copy(
            src_ref=source,
            dst_ref=target,
            send_sem=sent,
            recv_sem=received,
            device_id=to,
            device_id_type=MESH,
        )

    def lanes_of(n):
        return slice(n * 128, (n + 1) * 128)

    def first(n):
        if n % 2 == 0:
            source, to = dens.at[:, :, 1 - x_at, :, lanes_of(n)], x_peer
        else:
            source, to = dens.at[:, 1 - y_at, :, :, lanes_of(n)], y_peer
        return remote(source, first_in.at[n], first_send.at[n], first_recv.at[n], (g, to))

    def second(n):
        if n % 2 == 0:
            source, to = dens.at[:, 1 - y_at, x_at, :, lanes_of(n)], y_peer
        else:
            source, to = dens.at[:, y_at, 1 - x_at, :, lanes_of(n)], x_peer
        return remote(source, second_in.at[n], second_send.at[n], second_recv.at[n], (g, to))

    def third(n, step):
        to = at(4 * step)
        return remote(
            dens.at[to // 4, y_at, x_at, :, lanes_of(n)],
            third_in.at[n, step - 1],
            third_send.at[n, step - 1],
            third_recv.at[n, step - 1],
            (g, to),
        )

    for n in range(parts):
        first(n).start()

    share = remote(evec, ein, energy_send.at[0], energy_recv.at[0], (mirror, me))
    share.start()
    share.wait()
    etot[...] = evec[...] + ein[...]
    to_b = remote(etot.at[1], eback, energy_send.at[1], energy_recv.at[1], (g, y_peer))
    to_r = remote(etot.at[pl.ds(2, 2)], efar, energy_send.at[2], energy_recv.at[2], (g, r_id))

    @pl.when(even)
    def _():
        to_b.start()

    @pl.when(is_two == 0)
    def _():
        to_r.start()

    def take_first(n):
        first(n).wait_recv()
        if n % 2 == 0:
            dens[:, :, x_at, :, lanes_of(n)] += first_in[n]
        else:
            dens[:, y_at, :, :, lanes_of(n)] += first_in[n]
        second(n).start()

    def take_second(n):
        second(n).wait_recv()
        dens[:, y_at, x_at, :, lanes_of(n)] += second_in[n]
        for step in range(1, layers):
            third(n, step).start()

    for n in range(parts):
        take_first(n)
        if n >= 2:
            take_second(n - 2)
    for n in range(max(parts - 2, 0), parts):
        take_second(n)

    efin[...] = etot[...]

    @pl.when(even)
    def _():
        to_b.wait()
        efin[1] = eback[...]

    @pl.when(is_two == 0)
    def _():
        to_r.wait()
        efin[2:4] = efar[...]

    lane = lax.broadcasted_iota(jnp.int32, (1, 4), 1)
    energies = jnp.zeros((1, 4), jnp.float32)
    for s in range(4):
        energies = jnp.where(lane == s, -jnp.sum(efin[s]) / (width * width), energies)
    pairs_ref[...] = energies

    for n in range(parts):
        value = dens[z_at, y_at, x_at, :, lanes_of(n)]
        for step in range(1, layers):
            third(n, step).wait_recv()
            value = value + third_in[n, step - 1]
        density_ref[:, lanes_of(n)] = value / (count * STEPS)

    for n in range(parts):
        first(n).wait_send()
        second(n).wait_send()
        for step in range(1, layers):
            third(n, step).wait_send()

    @pl.loop(0, slices)
    def _(k):
        flow_col(k).wait_send()
        flow_other(k).wait_send()
        reflect(0, k).wait_send()
        reflect(1, k).wait_send()

        @pl.when(place == 0)
        def _():
            flow_down(k).wait_send()

        @pl.when(even)
        def _():
            reflect(2, k).wait_send()


def fused(count, ints, occ_energy, occ_window, virt_energy):
    width, depth = ints.shape[1:]
    slices, layers, slab = depth // SLICE, count // 4, width // count
    tiles, parts = width // TILE, width // 128
    dma = pltpu.SemaphoreType.DMA
    return pl.pallas_call(
        functools.partial(fused_kernel, count),
        out_shape=(
            jax.ShapeDtypeStruct((slab, width), jnp.float32),
            jax.ShapeDtypeStruct((1, STEPS), jnp.float32),
        ),
        in_specs=[
            pl.BlockSpec(memory_space=pl.ANY),
            pl.BlockSpec(memory_space=pltpu.SMEM),
            pl.BlockSpec(memory_space=pltpu.SMEM),
            pl.BlockSpec(memory_space=pltpu.VMEM),
        ],
        out_specs=(
            pl.BlockSpec(memory_space=pltpu.VMEM),
            pl.BlockSpec(memory_space=pltpu.VMEM),
        ),
        scratch_shapes=[
            pltpu.VMEM((4, slices, width, SLICE), jnp.bfloat16),
            pltpu.VMEM((3, slices, width, SLICE), jnp.bfloat16),
            pltpu.VMEM((3, 2 * tiles, width, TILE), jnp.float32),
            pltpu.VMEM((layers, 2, 2, slab, width), jnp.float32),
            pltpu.VMEM((2, 2, width, TILE), jnp.bfloat16),
            pltpu.VMEM((width, 128), jnp.float32),
            pltpu.VMEM((2 * tiles, 1, TILE), jnp.float32),
            pltpu.VMEM((parts, layers, 2, slab, 128), jnp.float32),
            pltpu.VMEM((parts, layers, slab, 128), jnp.float32),
            pltpu.VMEM((parts, layers - 1, slab, 128), jnp.float32),
            pltpu.VMEM((4, 8, 128), jnp.float32),
            pltpu.VMEM((4, 8, 128), jnp.float32),
            pltpu.VMEM((4, 8, 128), jnp.float32),
            pltpu.VMEM((8, 128), jnp.float32),
            pltpu.VMEM((2, 8, 128), jnp.float32),
            pltpu.VMEM((4, 8, 128), jnp.float32),
            dma((slices,)),
            dma((3, slices)),
            dma((3, slices)),
            dma((3, slices)),
            dma((3, slices)),
            dma((parts,)),
            dma((parts,)),
            dma((parts,)),
            dma((parts,)),
            dma((parts, layers - 1)),
            dma((parts, layers - 1)),
            dma((3,)),
            dma((3,)),
        ],
        compiler_params=pltpu.CompilerParams(
            collective_id=0, has_side_effects=True, vmem_limit_bytes=67043328
        ),
    )(ints[0], occ_energy, occ_window, virt_energy[None, :])


def fused_or_local(mesh, ints, occ_energy, occ_window, virt_energy):
    groups, blocks = mesh.shape["grp"], mesh.shape["blk"]
    occ_dev, width, depth = ints.shape
    fits = occ_dev == 1 and STEPS == 4 and groups % 2 == 0 and blocks % 4 == 0 and blocks >= 8
    fits = fits and width % TILE == 0 and width % (8 * blocks) == 0 and depth % SLICE == 0
    if fits:
        return fused(blocks, ints, occ_energy, occ_window, virt_energy)
    return local(ints, occ_energy, occ_window, virt_energy)


def solution(mesh):
    return jax.shard_map(
        functools.partial(fused_or_local, mesh),
        mesh=mesh,
        in_specs=(P("blk", "grp", None), P(), P(), P()),
        out_specs=(P(("grp", "blk"), None), P("blk", None)),
        check_vma=False,
    )
```

```python
import functools

import jax
import jax.numpy as jnp
from jax import lax
from jax.experimental import pallas as pl
from jax.experimental.pallas import tpu as pltpu
from jax.sharding import PartitionSpec as P

STEPS = 4
CHUNKS = 1
RELAY = False


def from_partner(block, axis, stride):
    count = lax.axis_size(axis)
    route = []
    for low in range(count):
        high = low | 1 << stride
        if high != low and high < count:
            route += [(low, high), (high, low)]
    return lax.ppermute(block, axis, route)


def shifted(shard, axis, by):
    peers = lax.axis_size(axis)
    return lax.ppermute(shard, axis, [(i, (i + by) % peers) for i in range(peers)])


def lookup_many(values_in, where_at):
    positions = jnp.arange(values_in.shape[0], dtype=jnp.int32)
    matches = positions[None, :] == where_at[:, None]
    return jnp.sum(
        jnp.where(matches, values_in[None, :], jnp.zeros_like(values_in)[None, :]), axis=1
    )


def fetched(pieces, block_index, block_count):
    if not RELAY or block_count % 4:
        return (
            [shifted(piece, "blk", -2) for piece in pieces],
            [shifted(piece, "blk", 1) for piece in pieces],
        )
    blocks = range(block_count)
    cross_y = [(c, c ^ 2) for c in blocks]
    down = [(c, (c - 4) % block_count) for c in blocks if c & 2]
    evens = [(c, c + 1) for c in blocks if c % 2 == 0]
    odds = [(c, (c + (-1 if c & 2 else 3)) % block_count) for c in blocks if c % 2]
    upper = (block_index & 2) != 0
    odd = (block_index & 1) != 0
    further, back = [], []
    for piece in pieces:
        over = lax.ppermute(piece, "blk", cross_y)
        direct = lax.ppermute(piece, "blk", evens)
        relayed = lax.ppermute(over, "blk", odds)
        further.append(jnp.where(upper, lax.ppermute(over, "blk", down), over))
        back.append(jnp.where(odd, direct, relayed))
    return further, back


def local(ints, occ_energy, occ_window, virt_energy):
    occ_dev = ints.shape[0]
    virt_width = ints.shape[1]
    occ_count = occ_window.shape[0]
    block_count = occ_count // occ_dev
    group_index = lax.axis_index("grp")
    block_index = lax.axis_index("blk")
    mirror_index = group_index + 1 - 2 * (group_index % 2)
    virt_own = lax.dynamic_slice_in_dim(virt_energy, group_index * virt_width, virt_width)
    virt_mirror = lax.dynamic_slice_in_dim(virt_energy, mirror_index * virt_width, virt_width)
    local_rows = jnp.arange(occ_dev, dtype=jnp.int32)

    def levels(offset):
        block = (block_index + offset) % block_count
        return lookup_many(occ_energy, lookup_many(occ_window, block * occ_dev + local_rows))

    occ_own, occ_back, occ_further = levels(0), levels(-1), levels(2)
    chunks = CHUNKS if virt_width % (16 * CHUNKS) == 0 else 1
    size = virt_width // chunks
    pieces = [ints[:, n * size : (n + 1) * size] for n in range(chunks)]
    mirror = from_partner(ints, "grp", 0)
    further_pieces, back_pieces = fetched(pieces, block_index, block_count)
    virt_pieces = [
        (virt_own[n * size : (n + 1) * size], virt_mirror[n * size : (n + 1) * size])
        for n in range(chunks)
    ]

    def tile(rows, cols, virt_cols, occ_rows, occ_cols):
        coupling = jnp.einsum("rap,tbp->rtab", rows, cols, preferred_element_type=jnp.float32)
        denominator = (
            virt_own[None, None, :, None]
            + virt_cols[None, None, None, :]
            - occ_rows[:, None, None, None]
            - occ_cols[None, :, None, None]
        )
        amplitude = coupling / denominator
        square = amplitude * amplitude
        energy = -jnp.sum(square * denominator, axis=(2, 3)) / (virt_width * virt_width)
        kept = lax.reduce_precision(amplitude, exponent_bits=8, mantissa_bits=7)
        high = kept.astype(jnp.bfloat16)
        low = (amplitude - kept).astype(jnp.bfloat16)
        main = jnp.einsum("rtab,rtcb->ac", high, high, preferred_element_type=jnp.float32)
        side = jnp.einsum("rtab,rtcb->ac", high, low, preferred_element_type=jnp.float32)
        return main, side, energy

    def add(one, other):
        return tuple(a + b for a, b in zip(one, other))

    zero = add(
        tile(ints, ints, virt_own, occ_own, occ_own),
        tile(ints, mirror, virt_mirror, occ_own, occ_own),
    )
    one = None
    for piece, (near, far) in zip(back_pieces, virt_pieces):
        part = add(
            tile(ints, piece, near, occ_own, occ_back),
            tile(ints, from_partner(piece, "grp", 0), far, occ_own, occ_back),
        )
        one = part if one is None else add(one, part)
    further = jnp.concatenate(further_pieces, axis=1)
    two = add(
        tile(further, ints, virt_own, occ_further, occ_own),
        tile(further, mirror, virt_mirror, occ_further, occ_own),
    )
    three = None
    for piece, (near, far) in zip(back_pieces, virt_pieces):
        part = add(
            tile(further, piece, near, occ_further, occ_back),
            tile(further, from_partner(piece, "grp", 0), far, occ_further, occ_back),
        )
        three = part if three is None else add(three, part)
    main, side = add(add(zero[:2], one[:2]), add(two[:2], three[:2]))
    density = main + side + side.T
    shares = lax.psum_scatter(density, "blk", scatter_dimension=0, tiled=True) / (
        occ_count * STEPS * occ_dev
    )
    sent = shifted(jnp.concatenate([two[2], three[2]], axis=1), "blk", 2)
    energies = jnp.concatenate([zero[2], one[2], sent], axis=1)
    return (shares, energies + from_partner(energies, "grp", 0))


MESH = pl.DeviceIdType.MESH
TILE = 256
SLICE = 256
ROWS = 64
NT = (((1,), (1,)), ((), ()))


def product(rows, cols):
    return lax.dot_general(rows, cols, NT, preferred_element_type=jnp.float32)


def fused_kernel(
    count,
    ints_ref,
    energy_ref,
    window_ref,
    virt_ref,
    density_ref,
    pairs_ref,
    buf,
    mir,
    acc,
    dens,
    split,
    rows_virt,
    cols_virt,
    first_in,
    second_in,
    third_in,
    evec,
    ein,
    etot,
    eback,
    efar,
    efin,
    load_sem,
    send_sem,
    recv_sem,
    mirror_send,
    mirror_recv,
    first_send,
    first_recv,
    second_send,
    second_recv,
    third_send,
    third_recv,
    energy_send,
    energy_recv,
):
    g = lax.axis_index("grp")
    me = lax.axis_index("blk")
    slices, width, depth = buf.shape[1:]
    layers = count // 4
    slab = dens.shape[3]
    tiles = width // TILE
    parts = width // 128
    place = me % 4
    x_at, y_at, z_at = me % 2, (me // 2) % 2, me // 4
    odd = place % 2
    even = odd == 0
    mirror = g + 1 - 2 * (g % 2)

    def at(offset):
        return (me + offset + count) % count

    x_peer = me + 1 - 2 * x_at
    y_peer = me + 2 - 4 * y_at
    is_two = (place // 2) * (1 - odd)
    col_to = at(1 - 2 * odd + 4 * (place // 3))
    other_to = at(2 - 4 * ((place + 3) // 4))
    other_slot = 2 + odd
    b_slot = 2 * (1 - odd)
    r_slot = 3 - 3 * is_two
    col_id = at(1 - 2 * ((place + 3) // 4) - 2 * is_two)
    b_id = at((1 - odd) * (2 - 4 * is_two))
    r_id = at(2 * odd + 4 * (1 - odd) * (1 - is_two))

    barrier = pltpu.get_barrier_semaphore()
    peers = [(g, x_peer), (mirror, me)]
    peers += [(g, at(o)) for o in (2, -2, 3, -3)]
    peers += [(g, at(4 * n)) for n in range(1, layers)]
    for peer in peers:
        pl.semaphore_signal(barrier, inc=1, device_id=peer, device_id_type=MESH)

    def load(k):
        return pltpu.make_async_copy(
            ints_ref.at[:, pl.ds(pl.multiple_of(k * depth, depth), depth)],
            buf.at[0, k],
            load_sem.at[k],
        )

    def flow(lane, k, slot, to):
        return pltpu.make_async_remote_copy(
            src_ref=buf.at[0, k],
            dst_ref=buf.at[slot, k],
            send_sem=send_sem.at[lane, k],
            recv_sem=recv_sem.at[lane, k],
            device_id=(g, to),
            device_id_type=MESH,
        )

    def flow_col(k):
        return flow(0, k, 1, col_to)

    def flow_other(k):
        return flow(1, k, other_slot, other_to)

    def flow_down(k):
        return flow(2, k, 3, at(-4))

    def reflect(slot, k):
        return pltpu.make_async_remote_copy(
            src_ref=buf.at[slot, k],
            dst_ref=mir.at[slot, k],
            send_sem=mirror_send.at[slot, k],
            recv_sem=mirror_recv.at[slot, k],
            device_id=(mirror, me),
            device_id_type=MESH,
        )

    @pl.loop(0, slices)
    def _(k):
        load(k).start()

    pl.semaphore_wait(barrier, len(peers))

    @pl.loop(0, slices)
    def _(k):
        load(k).wait()
        flow_col(k).start()
        flow_other(k).start()

        @pl.when(place == 0)
        def _():
            flow_down(k).start()

        reflect(0, k).start()

    def virt_row(group, n):
        return virt_ref[pl.ds(group * parts + n, 1), :]

    for n in range(parts):
        mine, theirs = virt_row(g, n), virt_row(mirror, n)
        lanes = slice(n % 2 * 128, (n % 2 + 1) * 128)
        cols_virt[n // 2, :, lanes] = mine
        cols_virt[tiles + n // 2, :, lanes] = theirs
        rows_virt[n * 128 : (n + 1) * 128, :] = jnp.transpose(jnp.broadcast_to(mine, (128, 128)))

    def level(index):
        return energy_ref[window_ref[index]]

    own_level, col_level, b_level, r_level = level(me), level(col_id), level(b_id), level(r_id)

    def clear(pair):
        @pl.loop(0, 2 * tiles)
        def _(n):
            acc[pair, n] = jnp.zeros(acc.shape[2:], jnp.float32)

    def couple_near(pair, row_slot, col_slot, k):
        rows = buf[row_slot, k]
        for n in range(tiles):
            acc[pair, n] += product(rows, buf[col_slot, k, n * TILE : (n + 1) * TILE, :])

    def couple_far(pair, row_slot, col_slot, k):
        rows = buf[row_slot, k]
        for n in range(tiles):
            acc[pair, tiles + n] += product(rows, mir[col_slot, k, n * TILE : (n + 1) * TILE, :])

    def amplitudes(pair, n, levels, energy_at, highs, lows):
        total = jnp.zeros((8, 128), jnp.float32)
        for r in range(width // ROWS):
            span = slice(r * ROWS, (r + 1) * ROWS)
            base = rows_virt[span, :] - levels
            for h in range(TILE // 128):
                lanes = slice(h * 128, (h + 1) * 128)
                coupling = acc[pair, n, span, lanes]
                amplitude = coupling / (base + cols_virt[n, :, lanes])
                term = amplitude * coupling
                total = total + jnp.sum(term.reshape(ROWS // 8, 8, 128), axis=0)
                high = amplitude.astype(jnp.bfloat16)
                highs[span, lanes] = high
                lows[span, lanes] = (amplitude - high.astype(jnp.float32)).astype(jnp.bfloat16)
        evec[energy_at] += total

    def slabs_of(start, stop):
        for s in range(start // slab, -(-stop // slab)):
            low, high = max(start, s * slab), min(stop, (s + 1) * slab)
            yield (s // 4, (s // 2) % 2, s % 2), low, high, s * slab

    def densities(n, highs, lows):
        start, stop = n * TILE, (n + 1) * TILE
        high, low = highs[:stop, :], lows[:stop, :]
        turn_high, turn_low = highs[start:stop, :], lows[start:stop, :]
        update = product(
            jnp.concatenate([high, high, low], axis=1),
            jnp.concatenate([turn_high, turn_low, turn_high], axis=1),
        )
        for where, low_row, high_row, origin in slabs_of(0, stop):
            dens[(*where, slice(low_row - origin, high_row - origin), slice(start, stop))] += (
                update[low_row:high_row]
            )

    def own_split(side):
        return split.at[side, 0], split.at[side, 1]

    def own_densities(side):
        for n in range(tiles):
            densities(n, *own_split(side))

    evec[...] = jnp.zeros(evec.shape, jnp.float32)
    dens[...] = jnp.zeros(dens.shape, jnp.float32)

    clear(0)

    @pl.loop(0, slices)
    def _(k):
        couple_near(0, 0, 0, k)

    @pl.loop(0, slices)
    def _(k):
        reflect(0, k).wait_recv()
        couple_far(0, 0, 0, k)

    amplitudes(0, 0, own_level + own_level, 0, *own_split(0))

    @pl.loop(1, 2 * tiles)
    def _(n):
        amplitudes(0, n, own_level + own_level, 0, *own_split(n % 2))
        own_densities((n + 1) % 2)

    own_densities((2 * tiles - 1) % 2)

    for pair in range(3):
        clear(pair)

    @pl.loop(0, slices)
    def _(k):
        flow_col(k).wait_recv()
        reflect(1, k).start()
        flow_other(k).wait_recv()

        @pl.when(even)
        def _():
            reflect(2, k).start()

        @pl.when(place == 0)
        def _():
            flow_down(k).wait_recv()

        couple_near(0, b_slot, 1, k)
        couple_near(1, r_slot, b_slot, k)
        couple_near(2, r_slot, 1, k)
        reflect(1, k).wait_recv()

        @pl.when(even)
        def _():
            reflect(2, k).wait_recv()

        couple_far(0, b_slot, 1, k)
        couple_far(1, r_slot, b_slot, k)
        couple_far(2, r_slot, 1, k)

    def levels_of(pair):
        return jnp.where(
            pair == 0,
            b_level + col_level,
            jnp.where(pair == 1, r_level + b_level, r_level + col_level),
        )

    def kept(t):
        pair, n = t // (2 * tiles), t % (2 * tiles)
        return mir.at[pair, n], mir.at[pair, 2 * tiles + n]

    last = tiles - 1
    amplitudes(0, 0, levels_of(0), 1, *kept(0))

    @pl.loop(1, 6 * tiles)
    def _(t):
        pair, n = t // (2 * tiles), t % (2 * tiles)
        amplitudes(pair, n, levels_of(pair), 1 + pair, *kept(t))
        densities(last, *kept(t - 1))

    densities(last, *kept(6 * tiles - 1))

    def turn(n, m):
        block = [
            dens[(*where, slice(low - origin, high - origin), slice(m * TILE, (m + 1) * TILE))]
            for where, low, high, origin in slabs_of(n * TILE, (n + 1) * TILE)
        ]
        turned = jnp.transpose(jnp.concatenate(block, axis=0))
        for where, low, high, origin in slabs_of(m * TILE, (m + 1) * TILE):
            dens[(*where, slice(low - origin, high - origin), slice(n * TILE, (n + 1) * TILE))] = (
                turned[low - m * TILE : high - m * TILE]
            )

    def remote(source, target, sent, received, to):
        return pltpu.make_async_remote_copy(
            src_ref=source,
            dst_ref=target,
            send_sem=sent,
            recv_sem=received,
            device_id=to,
            device_id_type=MESH,
        )

    def lanes_of(n):
        return slice(n * 128, (n + 1) * 128)

    def first(n):
        if n % 2 == 0:
            source, to = dens.at[:, :, 1 - x_at, :, lanes_of(n)], x_peer
        else:
            source, to = dens.at[:, 1 - y_at, :, :, lanes_of(n)], y_peer
        return remote(source, first_in.at[n], first_send.at[n], first_recv.at[n], (g, to))

    def second(n):
        if n % 2 == 0:
            source, to = dens.at[:, 1 - y_at, x_at, :, lanes_of(n)], y_peer
        else:
            source, to = dens.at[:, y_at, 1 - x_at, :, lanes_of(n)], x_peer
        return remote(source, second_in.at[n], second_send.at[n], second_recv.at[n], (g, to))

    def third(n, step):
        to = at(4 * step)
        return remote(
            dens.at[to // 4, y_at, x_at, :, lanes_of(n)],
            third_in.at[n, step - 1],
            third_send.at[n, step - 1],
            third_recv.at[n, step - 1],
            (g, to),
        )

    for n in (2 * last, 2 * last + 1):
        first(n).start()

    share = remote(evec, ein, energy_send.at[0], energy_recv.at[0], (mirror, me))
    share.start()
    for m in range(last):
        turn(m, last)
    to_b = remote(etot.at[1], eback, energy_send.at[1], energy_recv.at[1], (g, y_peer))
    to_r = remote(etot.at[pl.ds(2, 2)], efar, energy_send.at[2], energy_recv.at[2], (g, r_id))

    def take_first(n):
        first(n).wait_recv()
        if n % 2 == 0:
            dens[:, :, x_at, :, lanes_of(n)] += first_in[n]
        else:
            dens[:, y_at, :, :, lanes_of(n)] += first_in[n]
        second(n).start()

    def take_second(n):
        second(n).wait_recv()
        dens[:, y_at, x_at, :, lanes_of(n)] += second_in[n]
        for step in range(1, layers):
            third(n, step).start()

    waiting = [2 * last, 2 * last + 1]
    halfway = []
    for n in range(last - 1, -1, -1):

        @pl.loop(0, 6 * tiles)
        def _(t):
            densities(n, *kept(t))

        for m in (2 * n, 2 * n + 1):
            first(m).start()
        for m in range(n):
            turn(m, n)
        if n == last - 1:
            share.wait()
            etot[...] = evec[...] + ein[...]

            @pl.when(even)
            def _():
                to_b.start()

            @pl.when(is_two == 0)
            def _():
                to_r.start()

        for m in waiting:
            take_first(m)
        for m in halfway:
            take_second(m)
        waiting, halfway = [2 * n, 2 * n + 1], waiting
    for m in waiting:
        take_first(m)
    for m in halfway + waiting:
        take_second(m)

    efin[...] = etot[...]

    @pl.when(even)
    def _():
        to_b.wait()
        efin[1] = eback[...]

    @pl.when(is_two == 0)
    def _():
        to_r.wait()
        efin[2:4] = efar[...]

    lane = lax.broadcasted_iota(jnp.int32, (1, 4), 1)
    energies = jnp.zeros((1, 4), jnp.float32)
    for s in range(4):
        energies = jnp.where(lane == s, -jnp.sum(efin[s]) / (width * width), energies)
    pairs_ref[...] = energies

    for n in range(parts):
        value = dens[z_at, y_at, x_at, :, lanes_of(n)]
        for step in range(1, layers):
            third(n, step).wait_recv()
            value = value + third_in[n, step - 1]
        density_ref[:, lanes_of(n)] = value / (count * STEPS)

    for n in range(parts):
        first(n).wait_send()
        second(n).wait_send()
        for step in range(1, layers):
            third(n, step).wait_send()

    @pl.loop(0, slices)
    def _(k):
        flow_col(k).wait_send()
        flow_other(k).wait_send()
        reflect(0, k).wait_send()
        reflect(1, k).wait_send()

        @pl.when(place == 0)
        def _():
            flow_down(k).wait_send()

        @pl.when(even)
        def _():
            reflect(2, k).wait_send()


def fused(count, ints, occ_energy, occ_window, virt_energy):
    width, depth = ints.shape[1:]
    slices, layers, slab = depth // SLICE, count // 4, width // count
    tiles, parts = width // TILE, width // 128
    dma = pltpu.SemaphoreType.DMA
    return pl.pallas_call(
        functools.partial(fused_kernel, count),
        out_shape=(
            jax.ShapeDtypeStruct((slab, width), jnp.float32),
            jax.ShapeDtypeStruct((1, STEPS), jnp.float32),
        ),
        in_specs=[
            pl.BlockSpec(memory_space=pl.ANY),
            pl.BlockSpec(memory_space=pltpu.SMEM),
            pl.BlockSpec(memory_space=pltpu.SMEM),
            pl.BlockSpec(memory_space=pltpu.VMEM),
        ],
        out_specs=(
            pl.BlockSpec(memory_space=pltpu.VMEM),
            pl.BlockSpec(memory_space=pltpu.VMEM),
        ),
        scratch_shapes=[
            pltpu.VMEM((4, slices, width, SLICE), jnp.bfloat16),
            pltpu.VMEM((3, slices, width, SLICE), jnp.bfloat16),
            pltpu.VMEM((3, 2 * tiles, width, TILE), jnp.float32),
            pltpu.VMEM((layers, 2, 2, slab, width), jnp.float32),
            pltpu.VMEM((2, 2, width, TILE), jnp.bfloat16),
            pltpu.VMEM((width, 128), jnp.float32),
            pltpu.VMEM((2 * tiles, 1, TILE), jnp.float32),
            pltpu.VMEM((parts, layers, 2, slab, 128), jnp.float32),
            pltpu.VMEM((parts, layers, slab, 128), jnp.float32),
            pltpu.VMEM((parts, layers - 1, slab, 128), jnp.float32),
            pltpu.VMEM((4, 8, 128), jnp.float32),
            pltpu.VMEM((4, 8, 128), jnp.float32),
            pltpu.VMEM((4, 8, 128), jnp.float32),
            pltpu.VMEM((8, 128), jnp.float32),
            pltpu.VMEM((2, 8, 128), jnp.float32),
            pltpu.VMEM((4, 8, 128), jnp.float32),
            dma((slices,)),
            dma((3, slices)),
            dma((3, slices)),
            dma((3, slices)),
            dma((3, slices)),
            dma((parts,)),
            dma((parts,)),
            dma((parts,)),
            dma((parts,)),
            dma((parts, layers - 1)),
            dma((parts, layers - 1)),
            dma((3,)),
            dma((3,)),
        ],
        compiler_params=pltpu.CompilerParams(
            collective_id=0, has_side_effects=True, vmem_limit_bytes=67043328
        ),
    )(ints[0], occ_energy, occ_window, virt_energy.reshape(-1, 128))


def fused_or_local(mesh, ints, occ_energy, occ_window, virt_energy):
    groups, blocks = mesh.shape["grp"], mesh.shape["blk"]
    occ_dev, width, depth = ints.shape
    fits = occ_dev == 1 and STEPS == 4 and groups % 2 == 0 and blocks % 4 == 0 and blocks >= 8
    fits = fits and width % TILE == 0 and width % (8 * blocks) == 0 and depth % SLICE == 0
    fits = fits and width > TILE and depth // SLICE >= 4 * (width // TILE)
    if fits:
        return fused(blocks, ints, occ_energy, occ_window, virt_energy)
    return local(ints, occ_energy, occ_window, virt_energy)


def solution(mesh):
    return jax.shard_map(
        functools.partial(fused_or_local, mesh),
        mesh=mesh,
        in_specs=(P("blk", "grp", None), P(), P(), P()),
        out_specs=(P(("grp", "blk"), None), P("blk", None)),
        check_vma=False,
    )
```

```python
import functools

import jax
import jax.numpy as jnp
from jax import lax
from jax.experimental import pallas as pl
from jax.experimental.pallas import tpu as pltpu
from jax.sharding import PartitionSpec as P

STEPS = 4
CHUNKS = 1
RELAY = False


def from_partner(block, axis, stride):
    count = lax.axis_size(axis)
    route = []
    for low in range(count):
        high = low | 1 << stride
        if high != low and high < count:
            route += [(low, high), (high, low)]
    return lax.ppermute(block, axis, route)


def shifted(shard, axis, by):
    peers = lax.axis_size(axis)
    return lax.ppermute(shard, axis, [(i, (i + by) % peers) for i in range(peers)])


def lookup_many(values_in, where_at):
    positions = jnp.arange(values_in.shape[0], dtype=jnp.int32)
    matches = positions[None, :] == where_at[:, None]
    return jnp.sum(
        jnp.where(matches, values_in[None, :], jnp.zeros_like(values_in)[None, :]), axis=1
    )


def fetched(pieces, block_index, block_count):
    if not RELAY or block_count % 4:
        return (
            [shifted(piece, "blk", -2) for piece in pieces],
            [shifted(piece, "blk", 1) for piece in pieces],
        )
    blocks = range(block_count)
    cross_y = [(c, c ^ 2) for c in blocks]
    down = [(c, (c - 4) % block_count) for c in blocks if c & 2]
    evens = [(c, c + 1) for c in blocks if c % 2 == 0]
    odds = [(c, (c + (-1 if c & 2 else 3)) % block_count) for c in blocks if c % 2]
    upper = (block_index & 2) != 0
    odd = (block_index & 1) != 0
    further, back = [], []
    for piece in pieces:
        over = lax.ppermute(piece, "blk", cross_y)
        direct = lax.ppermute(piece, "blk", evens)
        relayed = lax.ppermute(over, "blk", odds)
        further.append(jnp.where(upper, lax.ppermute(over, "blk", down), over))
        back.append(jnp.where(odd, direct, relayed))
    return further, back


def local(ints, occ_energy, occ_window, virt_energy):
    occ_dev = ints.shape[0]
    virt_width = ints.shape[1]
    occ_count = occ_window.shape[0]
    block_count = occ_count // occ_dev
    group_index = lax.axis_index("grp")
    block_index = lax.axis_index("blk")
    mirror_index = group_index + 1 - 2 * (group_index % 2)
    virt_own = lax.dynamic_slice_in_dim(virt_energy, group_index * virt_width, virt_width)
    virt_mirror = lax.dynamic_slice_in_dim(virt_energy, mirror_index * virt_width, virt_width)
    local_rows = jnp.arange(occ_dev, dtype=jnp.int32)

    def levels(offset):
        block = (block_index + offset) % block_count
        return lookup_many(occ_energy, lookup_many(occ_window, block * occ_dev + local_rows))

    occ_own, occ_back, occ_further = levels(0), levels(-1), levels(2)
    chunks = CHUNKS if virt_width % (16 * CHUNKS) == 0 else 1
    size = virt_width // chunks
    pieces = [ints[:, n * size : (n + 1) * size] for n in range(chunks)]
    mirror = from_partner(ints, "grp", 0)
    further_pieces, back_pieces = fetched(pieces, block_index, block_count)
    virt_pieces = [
        (virt_own[n * size : (n + 1) * size], virt_mirror[n * size : (n + 1) * size])
        for n in range(chunks)
    ]

    def tile(rows, cols, virt_cols, occ_rows, occ_cols):
        coupling = jnp.einsum("rap,tbp->rtab", rows, cols, preferred_element_type=jnp.float32)
        denominator = (
            virt_own[None, None, :, None]
            + virt_cols[None, None, None, :]
            - occ_rows[:, None, None, None]
            - occ_cols[None, :, None, None]
        )
        amplitude = coupling / denominator
        square = amplitude * amplitude
        energy = -jnp.sum(square * denominator, axis=(2, 3)) / (virt_width * virt_width)
        kept = lax.reduce_precision(amplitude, exponent_bits=8, mantissa_bits=7)
        high = kept.astype(jnp.bfloat16)
        low = (amplitude - kept).astype(jnp.bfloat16)
        main = jnp.einsum("rtab,rtcb->ac", high, high, preferred_element_type=jnp.float32)
        side = jnp.einsum("rtab,rtcb->ac", high, low, preferred_element_type=jnp.float32)
        return main, side, energy

    def add(one, other):
        return tuple(a + b for a, b in zip(one, other))

    zero = add(
        tile(ints, ints, virt_own, occ_own, occ_own),
        tile(ints, mirror, virt_mirror, occ_own, occ_own),
    )
    one = None
    for piece, (near, far) in zip(back_pieces, virt_pieces):
        part = add(
            tile(ints, piece, near, occ_own, occ_back),
            tile(ints, from_partner(piece, "grp", 0), far, occ_own, occ_back),
        )
        one = part if one is None else add(one, part)
    further = jnp.concatenate(further_pieces, axis=1)
    two = add(
        tile(further, ints, virt_own, occ_further, occ_own),
        tile(further, mirror, virt_mirror, occ_further, occ_own),
    )
    three = None
    for piece, (near, far) in zip(back_pieces, virt_pieces):
        part = add(
            tile(further, piece, near, occ_further, occ_back),
            tile(further, from_partner(piece, "grp", 0), far, occ_further, occ_back),
        )
        three = part if three is None else add(three, part)
    main, side = add(add(zero[:2], one[:2]), add(two[:2], three[:2]))
    density = main + side + side.T
    shares = lax.psum_scatter(density, "blk", scatter_dimension=0, tiled=True) / (
        occ_count * STEPS * occ_dev
    )
    sent = shifted(jnp.concatenate([two[2], three[2]], axis=1), "blk", 2)
    energies = jnp.concatenate([zero[2], one[2], sent], axis=1)
    return (shares, energies + from_partner(energies, "grp", 0))


MESH = pl.DeviceIdType.MESH
TILE = 256
SLICE = 256
ROWS = 64
NT = (((1,), (1,)), ((), ()))


def product(rows, cols):
    return lax.dot_general(rows, cols, NT, preferred_element_type=jnp.float32)


def fused_kernel(
    count,
    ints_ref,
    energy_in,
    window_in,
    virt_in,
    density_ref,
    pairs_ref,
    energy_ref,
    window_ref,
    virt_ref,
    buf,
    mir,
    acc,
    dens,
    split,
    rows_virt,
    cols_virt,
    first_in,
    second_in,
    third_in,
    evec,
    ein,
    etot,
    eback,
    efar,
    efin,
    small_sem,
    load_sem,
    send_sem,
    recv_sem,
    mirror_send,
    mirror_recv,
    first_send,
    first_recv,
    second_send,
    second_recv,
    third_send,
    third_recv,
    energy_send,
    energy_recv,
):
    g = lax.axis_index("grp")
    me = lax.axis_index("blk")
    slices, width, depth = buf.shape[1:]
    layers = count // 4
    slab = dens.shape[3]
    tiles = width // TILE
    parts = width // 128
    place = me % 4
    x_at, y_at, z_at = me % 2, (me // 2) % 2, me // 4
    odd = place % 2
    even = odd == 0
    mirror = g + 1 - 2 * (g % 2)

    def at(offset):
        return (me + offset + count) % count

    x_peer = me + 1 - 2 * x_at
    y_peer = me + 2 - 4 * y_at
    is_two = (place // 2) * (1 - odd)
    col_to = at(1 - 2 * odd + 4 * (place // 3))
    other_to = at(2 - 4 * ((place + 3) // 4))
    other_slot = 2 + odd
    b_slot = 2 * (1 - odd)
    r_slot = 3 - 3 * is_two
    col_id = at(1 - 2 * ((place + 3) // 4) - 2 * is_two)
    b_id = at((1 - odd) * (2 - 4 * is_two))
    r_id = at(2 * odd + 4 * (1 - odd) * (1 - is_two))

    barrier = pltpu.get_barrier_semaphore()
    peers = [(g, x_peer), (mirror, me)]
    peers += [(g, at(o)) for o in (2, -2, 3, -3)]
    peers += [(g, at(4 * n)) for n in range(1, layers)]
    for peer in peers:
        pl.semaphore_signal(barrier, inc=1, device_id=peer, device_id_type=MESH)

    def load(k):
        return pltpu.make_async_copy(
            ints_ref.at[:, pl.ds(pl.multiple_of(k * depth, depth), depth)],
            buf.at[0, k],
            load_sem.at[k],
        )

    def flow(lane, k, slot, to):
        return pltpu.make_async_remote_copy(
            src_ref=buf.at[0, k],
            dst_ref=buf.at[slot, k],
            send_sem=send_sem.at[lane, k],
            recv_sem=recv_sem.at[lane, k],
            device_id=(g, to),
            device_id_type=MESH,
        )

    def flow_col(k):
        return flow(0, k, 1, col_to)

    def flow_other(k):
        return flow(1, k, other_slot, other_to)

    def flow_down(k):
        return flow(2, k, 3, at(-4))

    def reflect(slot, k):
        return pltpu.make_async_remote_copy(
            src_ref=buf.at[slot, k],
            dst_ref=mir.at[slot, k],
            send_sem=mirror_send.at[slot, k],
            recv_sem=mirror_recv.at[slot, k],
            device_id=(mirror, me),
            device_id_type=MESH,
        )

    small = [
        pltpu.make_async_copy(source, target, small_sem.at[n])
        for n, (source, target) in enumerate(
            ((energy_in, energy_ref), (window_in, window_ref), (virt_in, virt_ref))
        )
    ]

    @pl.loop(0, slices)
    def _(k):
        load(k).start()

    for copy in small:
        copy.start()

    pl.semaphore_wait(barrier, len(peers))

    @pl.loop(0, slices)
    def _(k):
        load(k).wait()
        flow_col(k).start()
        flow_other(k).start()

        @pl.when(place == 0)
        def _():
            flow_down(k).start()

        reflect(0, k).start()

    for copy in small:
        copy.wait()

    def virt_row(group, n):
        return virt_ref[pl.ds(group * parts + n, 1), :]

    for n in range(parts):
        mine, theirs = virt_row(g, n), virt_row(mirror, n)
        lanes = slice(n % 2 * 128, (n % 2 + 1) * 128)
        cols_virt[n // 2, :, lanes] = mine
        cols_virt[tiles + n // 2, :, lanes] = theirs
        rows_virt[n * 128 : (n + 1) * 128, :] = jnp.transpose(jnp.broadcast_to(mine, (128, 128)))

    def level(index):
        return energy_ref[window_ref[index]]

    own_level, col_level, b_level, r_level = level(me), level(col_id), level(b_id), level(r_id)

    def clear(pair):
        @pl.loop(0, 2 * tiles)
        def _(n):
            acc[pair, n] = jnp.zeros(acc.shape[2:], jnp.float32)

    def couple(pair, row_slot, k, cols, first_at):
        for n in range(tiles):
            side = cols[n * TILE : (n + 1) * TILE, :]
            for r in range(0, width, TILE):
                rows = slice(r, r + TILE)
                acc[pair, first_at + n, rows] += product(buf[row_slot, k, rows], side)

    def couple_near(pair, row_slot, col_slot, k):
        couple(pair, row_slot, k, buf.at[col_slot, k], 0)

    def couple_far(pair, row_slot, col_slot, k):
        couple(pair, row_slot, k, mir.at[col_slot, k], tiles)

    def amplitudes(pair, n, levels, energy_at, highs, lows):
        total = jnp.zeros((8, 128), jnp.float32)
        shifted_cols = [
            cols_virt[n, :, h * 128 : (h + 1) * 128] - levels for h in range(TILE // 128)
        ]
        for r in range(width // ROWS):
            span = slice(r * ROWS, (r + 1) * ROWS)
            base = rows_virt[span, :]
            for h in range(TILE // 128):
                lanes = slice(h * 128, (h + 1) * 128)
                coupling = acc[pair, n, span, lanes]
                amplitude = coupling / (base + shifted_cols[h])
                term = amplitude * coupling
                total = total + jnp.sum(term.reshape(ROWS // 8, 8, 128), axis=0)
                high = amplitude.astype(jnp.bfloat16)
                highs[span, lanes] = high
                lows[span, lanes] = (amplitude - high.astype(jnp.float32)).astype(jnp.bfloat16)
        evec[energy_at] += total

    def slabs_of(start, stop):
        for s in range(start // slab, -(-stop // slab)):
            low, high = max(start, s * slab), min(stop, (s + 1) * slab)
            yield (s // 4, (s // 2) % 2, s % 2), low, high, s * slab

    def densities(n, *splits, step=None):
        start, stop = n * TILE, (n + 1) * TILE
        step = step or TILE
        for first_row in range(0, stop, step):
            end_row = first_row + step
            update = None
            for highs, lows in splits:
                high, low = highs[first_row:end_row, :], lows[first_row:end_row, :]
                turn_high, turn_low = highs[start:stop, :], lows[start:stop, :]
                part = product(
                    jnp.concatenate([high, high, low], axis=1),
                    jnp.concatenate([turn_high, turn_low, turn_high], axis=1),
                )
                update = part if update is None else update + part
            for where, low_row, high_row, origin in slabs_of(first_row, end_row):
                dens[
                    (*where, slice(low_row - origin, high_row - origin), slice(start, stop))
                ] += update[low_row - first_row : high_row - first_row]

    evec[...] = jnp.zeros(evec.shape, jnp.float32)
    dens[...] = jnp.zeros(dens.shape, jnp.float32)

    clear(0)

    @pl.loop(0, slices)
    def _(k):
        couple_near(0, 0, 0, k)

    @pl.loop(0, slices)
    def _(k):
        reflect(0, k).wait_recv()
        couple_far(0, 0, 0, k)

    @pl.loop(0, 2 * tiles)
    def _(n):
        amplitudes(0, n, own_level + own_level, 0, split.at[0], split.at[1])
        for m in range(tiles):
            densities(m, (split.at[0], split.at[1]))

    for pair in range(3):
        clear(pair)

    @pl.loop(0, slices)
    def _(k):
        flow_col(k).wait_recv()
        reflect(1, k).start()
        flow_other(k).wait_recv()

        @pl.when(even)
        def _():
            reflect(2, k).start()

        @pl.when(place == 0)
        def _():
            flow_down(k).wait_recv()

        couple_near(0, b_slot, 1, k)
        couple_near(1, r_slot, b_slot, k)
        couple_near(2, r_slot, 1, k)
        reflect(1, k).wait_recv()

        @pl.when(even)
        def _():
            reflect(2, k).wait_recv()

        couple_far(0, b_slot, 1, k)
        couple_far(1, r_slot, b_slot, k)
        couple_far(2, r_slot, 1, k)

    @pl.loop(0, slices)
    def _(k):
        reflect(1, k).wait_send()

        @pl.when(even)
        def _():
            reflect(2, k).wait_send()

    def levels_of(pair):
        return jnp.where(
            pair == 0,
            b_level + col_level,
            jnp.where(pair == 1, r_level + b_level, r_level + col_level),
        )

    def kept(half, store):
        first_slot = store.shape[0] - 3
        slot, at_slice = half // (slices // 2), half % (slices // 2)
        return store.at[first_slot + slot, 2 * at_slice], store.at[first_slot + slot, 2 * at_slice + 1]

    def finish(t, highs, lows):
        pair, n = t // (2 * tiles), t % (2 * tiles)
        amplitudes(pair, n, levels_of(pair), 1 + pair, highs, lows)

    last = tiles - 1
    halves = 3 * tiles
    finish(0, *kept(0, mir))

    @pl.loop(0, halves - 1)
    def _(half):
        finish(2 * half + 1, *kept(half, buf))
        densities(last, kept(half, mir))
        finish(2 * half + 2, *kept(half + 1, mir))
        densities(last, kept(half, buf))

    finish(6 * tiles - 1, *kept(halves - 1, buf))
    densities(last, kept(halves - 1, mir))
    densities(last, kept(halves - 1, buf))

    def turn(n, m):
        block = [
            dens[(*where, slice(low - origin, high - origin), slice(m * TILE, (m + 1) * TILE))]
            for where, low, high, origin in slabs_of(n * TILE, (n + 1) * TILE)
        ]
        turned = jnp.transpose(jnp.concatenate(block, axis=0))
        for where, low, high, origin in slabs_of(m * TILE, (m + 1) * TILE):
            dens[(*where, slice(low - origin, high - origin), slice(n * TILE, (n + 1) * TILE))] = (
                turned[low - m * TILE : high - m * TILE]
            )

    def remote(source, target, sent, received, to):
        return pltpu.make_async_remote_copy(
            src_ref=source,
            dst_ref=target,
            send_sem=sent,
            recv_sem=received,
            device_id=to,
            device_id_type=MESH,
        )

    def lanes_of(n):
        return slice(n * 128, (n + 1) * 128)

    def first(n):
        if n % 2 == 0:
            source, to = dens.at[:, :, 1 - x_at, :, lanes_of(n)], x_peer
        else:
            source, to = dens.at[:, 1 - y_at, :, :, lanes_of(n)], y_peer
        return remote(source, first_in.at[n], first_send.at[n], first_recv.at[n], (g, to))

    def second(n):
        if n % 2 == 0:
            source, to = dens.at[:, 1 - y_at, x_at, :, lanes_of(n)], y_peer
        else:
            source, to = dens.at[:, y_at, 1 - x_at, :, lanes_of(n)], x_peer
        return remote(source, second_in.at[n], second_send.at[n], second_recv.at[n], (g, to))

    def third(n, step):
        to = at(4 * step)
        return remote(
            dens.at[to // 4, y_at, x_at, :, lanes_of(n)],
            third_in.at[n, step - 1],
            third_send.at[n, step - 1],
            third_recv.at[n, step - 1],
            (g, to),
        )

    for n in (2 * last, 2 * last + 1):
        first(n).start()

    share = remote(evec, ein, energy_send.at[0], energy_recv.at[0], (mirror, me))
    share.start()
    for m in range(last):
        turn(m, last)
    to_b = remote(etot.at[1], eback, energy_send.at[1], energy_recv.at[1], (g, y_peer))
    to_r = remote(etot.at[pl.ds(2, 2)], efar, energy_send.at[2], energy_recv.at[2], (g, r_id))

    def take_first(n):
        first(n).wait_recv()
        if n % 2 == 0:
            dens[:, :, x_at, :, lanes_of(n)] += first_in[n]
        else:
            dens[:, y_at, :, :, lanes_of(n)] += first_in[n]
        second(n).start()

    def take_second(n):
        second(n).wait_recv()
        dens[:, y_at, x_at, :, lanes_of(n)] += second_in[n]
        for step in range(1, layers):
            third(n, step).start()

    waiting = [2 * last, 2 * last + 1]
    halfway = []
    for n in range(last - 1, -1, -1):

        @pl.loop(0, 3)
        def _(third_of):
            densities(
                n,
                *(
                    kept(third_of * tiles + step, store)
                    for step in range(tiles)
                    for store in (mir, buf)
                ),
            )

        for m in (2 * n, 2 * n + 1):
            first(m).start()
        for m in range(n):
            turn(m, n)
        if n == last - 1:
            share.wait()
            etot[...] = evec[...] + ein[...]

            @pl.when(even)
            def _():
                to_b.start()

            @pl.when(is_two == 0)
            def _():
                to_r.start()

        for m in waiting:
            take_first(m)
        for m in halfway:
            take_second(m)
        waiting, halfway = [2 * n, 2 * n + 1], waiting
    for m in waiting:
        take_first(m)
    for m in halfway + waiting:
        take_second(m)

    efin[...] = etot[...]

    @pl.when(even)
    def _():
        to_b.wait()
        efin[1] = eback[...]

    @pl.when(is_two == 0)
    def _():
        to_r.wait()
        efin[2:4] = efar[...]

    lane = lax.broadcasted_iota(jnp.int32, (1, 4), 1)
    energies = jnp.zeros((1, 4), jnp.float32)
    for s in range(4):
        energies = jnp.where(lane == s, -jnp.sum(efin[s]) / (width * width), energies)
    pairs_ref[...] = energies

    for n in range(parts):
        value = dens[z_at, y_at, x_at, :, lanes_of(n)]
        for step in range(1, layers):
            third(n, step).wait_recv()
            value = value + third_in[n, step - 1]
        density_ref[:, lanes_of(n)] = value / (count * STEPS)

    for n in range(parts):
        first(n).wait_send()
        second(n).wait_send()
        for step in range(1, layers):
            third(n, step).wait_send()

    @pl.loop(0, slices)
    def _(k):
        flow_col(k).wait_send()
        flow_other(k).wait_send()
        reflect(0, k).wait_send()

        @pl.when(place == 0)
        def _():
            flow_down(k).wait_send()


def fused(count, ints, occ_energy, occ_window, virt_energy):
    width, depth = ints.shape[1:]
    slices, layers, slab = depth // SLICE, count // 4, width // count
    tiles, parts = width // TILE, width // 128
    dma = pltpu.SemaphoreType.DMA
    return pl.pallas_call(
        functools.partial(fused_kernel, count),
        out_shape=(
            jax.ShapeDtypeStruct((slab, width), jnp.float32),
            jax.ShapeDtypeStruct((1, STEPS), jnp.float32),
        ),
        in_specs=[
            pl.BlockSpec(memory_space=pl.ANY),
            pl.BlockSpec(memory_space=pl.ANY),
            pl.BlockSpec(memory_space=pl.ANY),
            pl.BlockSpec(memory_space=pl.ANY),
        ],
        out_specs=(
            pl.BlockSpec(memory_space=pltpu.VMEM),
            pl.BlockSpec(memory_space=pltpu.VMEM),
        ),
        scratch_shapes=[
            pltpu.SMEM(occ_energy.shape, jnp.float32),
            pltpu.SMEM(occ_window.shape, jnp.int32),
            pltpu.VMEM((virt_energy.shape[0] // 128, 128), jnp.float32),
            pltpu.VMEM((4, slices, width, SLICE), jnp.bfloat16),
            pltpu.VMEM((3, slices, width, SLICE), jnp.bfloat16),
            pltpu.VMEM((3, 2 * tiles, width, TILE), jnp.float32),
            pltpu.VMEM((layers, 2, 2, slab, width), jnp.float32),
            pltpu.VMEM((2, width, TILE), jnp.bfloat16),
            pltpu.VMEM((width, 128), jnp.float32),
            pltpu.VMEM((2 * tiles, 1, TILE), jnp.float32),
            pltpu.VMEM((parts, layers, 2, slab, 128), jnp.float32),
            pltpu.VMEM((parts, layers, slab, 128), jnp.float32),
            pltpu.VMEM((parts, layers - 1, slab, 128), jnp.float32),
            pltpu.VMEM((4, 8, 128), jnp.float32),
            pltpu.VMEM((4, 8, 128), jnp.float32),
            pltpu.VMEM((4, 8, 128), jnp.float32),
            pltpu.VMEM((8, 128), jnp.float32),
            pltpu.VMEM((2, 8, 128), jnp.float32),
            pltpu.VMEM((4, 8, 128), jnp.float32),
            dma((3,)),
            dma((slices,)),
            dma((3, slices)),
            dma((3, slices)),
            dma((3, slices)),
            dma((3, slices)),
            dma((parts,)),
            dma((parts,)),
            dma((parts,)),
            dma((parts,)),
            dma((parts, layers - 1)),
            dma((parts, layers - 1)),
            dma((3,)),
            dma((3,)),
        ],
        compiler_params=pltpu.CompilerParams(
            collective_id=0, has_side_effects=True, vmem_limit_bytes=67043328
        ),
    )(ints[0], occ_energy, occ_window, virt_energy.reshape(-1, 128))


def fused_or_local(mesh, ints, occ_energy, occ_window, virt_energy):
    groups, blocks = mesh.shape["grp"], mesh.shape["blk"]
    occ_dev, width, depth = ints.shape
    fits = occ_dev == 1 and STEPS == 4 and groups % 2 == 0 and blocks % 4 == 0 and blocks >= 8
    fits = fits and width % TILE == 0 and width % (8 * blocks) == 0 and depth % SLICE == 0
    fits = fits and width > TILE and depth // SLICE >= 4 * (width // TILE)
    if fits:
        return fused(blocks, ints, occ_energy, occ_window, virt_energy)
    return local(ints, occ_energy, occ_window, virt_energy)


def solution(mesh):
    return jax.shard_map(
        functools.partial(fused_or_local, mesh),
        mesh=mesh,
        in_specs=(P("blk", "grp", None), P(), P(), P()),
        out_specs=(P(("grp", "blk"), None), P("blk", None)),
        check_vma=False,
    )
```

```python
import functools

import jax
import jax.numpy as jnp
from jax import lax
from jax.experimental import pallas as pl
from jax.experimental.pallas import tpu as pltpu
from jax.sharding import PartitionSpec as P

STEPS = 4
CHUNKS = 1
RELAY = False


def from_partner(block, axis, stride):
    count = lax.axis_size(axis)
    route = []
    for low in range(count):
        high = low | 1 << stride
        if high != low and high < count:
            route += [(low, high), (high, low)]
    return lax.ppermute(block, axis, route)


def shifted(shard, axis, by):
    peers = lax.axis_size(axis)
    return lax.ppermute(shard, axis, [(i, (i + by) % peers) for i in range(peers)])


def lookup_many(values_in, where_at):
    positions = jnp.arange(values_in.shape[0], dtype=jnp.int32)
    matches = positions[None, :] == where_at[:, None]
    return jnp.sum(
        jnp.where(matches, values_in[None, :], jnp.zeros_like(values_in)[None, :]), axis=1
    )


def fetched(pieces, block_index, block_count):
    if not RELAY or block_count % 4:
        return (
            [shifted(piece, "blk", -2) for piece in pieces],
            [shifted(piece, "blk", 1) for piece in pieces],
        )
    blocks = range(block_count)
    cross_y = [(c, c ^ 2) for c in blocks]
    down = [(c, (c - 4) % block_count) for c in blocks if c & 2]
    evens = [(c, c + 1) for c in blocks if c % 2 == 0]
    odds = [(c, (c + (-1 if c & 2 else 3)) % block_count) for c in blocks if c % 2]
    upper = (block_index & 2) != 0
    odd = (block_index & 1) != 0
    further, back = [], []
    for piece in pieces:
        over = lax.ppermute(piece, "blk", cross_y)
        direct = lax.ppermute(piece, "blk", evens)
        relayed = lax.ppermute(over, "blk", odds)
        further.append(jnp.where(upper, lax.ppermute(over, "blk", down), over))
        back.append(jnp.where(odd, direct, relayed))
    return further, back


def local(ints, occ_energy, occ_window, virt_energy):
    occ_dev = ints.shape[0]
    virt_width = ints.shape[1]
    occ_count = occ_window.shape[0]
    block_count = occ_count // occ_dev
    group_index = lax.axis_index("grp")
    block_index = lax.axis_index("blk")
    mirror_index = group_index + 1 - 2 * (group_index % 2)
    virt_own = lax.dynamic_slice_in_dim(virt_energy, group_index * virt_width, virt_width)
    virt_mirror = lax.dynamic_slice_in_dim(virt_energy, mirror_index * virt_width, virt_width)
    local_rows = jnp.arange(occ_dev, dtype=jnp.int32)

    def levels(offset):
        block = (block_index + offset) % block_count
        return lookup_many(occ_energy, lookup_many(occ_window, block * occ_dev + local_rows))

    occ_own, occ_back, occ_further = levels(0), levels(-1), levels(2)
    chunks = CHUNKS if virt_width % (16 * CHUNKS) == 0 else 1
    size = virt_width // chunks
    pieces = [ints[:, n * size : (n + 1) * size] for n in range(chunks)]
    mirror = from_partner(ints, "grp", 0)
    further_pieces, back_pieces = fetched(pieces, block_index, block_count)
    virt_pieces = [
        (virt_own[n * size : (n + 1) * size], virt_mirror[n * size : (n + 1) * size])
        for n in range(chunks)
    ]

    def tile(rows, cols, virt_cols, occ_rows, occ_cols):
        coupling = jnp.einsum("rap,tbp->rtab", rows, cols, preferred_element_type=jnp.float32)
        denominator = (
            virt_own[None, None, :, None]
            + virt_cols[None, None, None, :]
            - occ_rows[:, None, None, None]
            - occ_cols[None, :, None, None]
        )
        amplitude = coupling / denominator
        square = amplitude * amplitude
        energy = -jnp.sum(square * denominator, axis=(2, 3)) / (virt_width * virt_width)
        kept = lax.reduce_precision(amplitude, exponent_bits=8, mantissa_bits=7)
        high = kept.astype(jnp.bfloat16)
        low = (amplitude - kept).astype(jnp.bfloat16)
        main = jnp.einsum("rtab,rtcb->ac", high, high, preferred_element_type=jnp.float32)
        side = jnp.einsum("rtab,rtcb->ac", high, low, preferred_element_type=jnp.float32)
        return main, side, energy

    def add(one, other):
        return tuple(a + b for a, b in zip(one, other))

    zero = add(
        tile(ints, ints, virt_own, occ_own, occ_own),
        tile(ints, mirror, virt_mirror, occ_own, occ_own),
    )
    one = None
    for piece, (near, far) in zip(back_pieces, virt_pieces):
        part = add(
            tile(ints, piece, near, occ_own, occ_back),
            tile(ints, from_partner(piece, "grp", 0), far, occ_own, occ_back),
        )
        one = part if one is None else add(one, part)
    further = jnp.concatenate(further_pieces, axis=1)
    two = add(
        tile(further, ints, virt_own, occ_further, occ_own),
        tile(further, mirror, virt_mirror, occ_further, occ_own),
    )
    three = None
    for piece, (near, far) in zip(back_pieces, virt_pieces):
        part = add(
            tile(further, piece, near, occ_further, occ_back),
            tile(further, from_partner(piece, "grp", 0), far, occ_further, occ_back),
        )
        three = part if three is None else add(three, part)
    main, side = add(add(zero[:2], one[:2]), add(two[:2], three[:2]))
    density = main + side + side.T
    shares = lax.psum_scatter(density, "blk", scatter_dimension=0, tiled=True) / (
        occ_count * STEPS * occ_dev
    )
    sent = shifted(jnp.concatenate([two[2], three[2]], axis=1), "blk", 2)
    energies = jnp.concatenate([zero[2], one[2], sent], axis=1)
    return (shares, energies + from_partner(energies, "grp", 0))


MESH = pl.DeviceIdType.MESH
TILE = 256
SLICE = 256
ROWS = 64
NT = (((1,), (1,)), ((), ()))


def product(rows, cols):
    return lax.dot_general(rows, cols, NT, preferred_element_type=jnp.float32)


def fused_kernel(
    count,
    ints_ref,
    energy_in,
    window_in,
    virt_in,
    density_ref,
    pairs_ref,
    energy_ref,
    window_ref,
    virt_ref,
    buf,
    mir,
    acc,
    dens,
    split,
    rows_virt,
    cols_virt,
    first_in,
    second_in,
    third_in,
    evec,
    ein,
    etot,
    eback,
    efar,
    efin,
    small_sem,
    load_sem,
    send_sem,
    recv_sem,
    mirror_send,
    mirror_recv,
    first_send,
    first_recv,
    second_send,
    second_recv,
    third_send,
    third_recv,
    energy_send,
    energy_recv,
):
    g = lax.axis_index("grp")
    me = lax.axis_index("blk")
    slices, width, depth = buf.shape[1:]
    layers = count // 4
    slab = dens.shape[3]
    tiles = width // TILE
    parts = width // 128
    place = me % 4
    x_at, y_at, z_at = me % 2, (me // 2) % 2, me // 4
    odd = place % 2
    even = odd == 0
    mirror = g + 1 - 2 * (g % 2)

    def at(offset):
        return (me + offset + count) % count

    x_peer = me + 1 - 2 * x_at
    y_peer = me + 2 - 4 * y_at
    is_two = (place // 2) * (1 - odd)
    col_to = at(1 - 2 * odd + 4 * (place // 3))
    other_to = at(2 - 4 * ((place + 3) // 4))
    other_slot = 2 + odd
    b_slot = 2 * (1 - odd)
    r_slot = 3 - 3 * is_two
    col_id = at(1 - 2 * ((place + 3) // 4) - 2 * is_two)
    b_id = at((1 - odd) * (2 - 4 * is_two))
    r_id = at(2 * odd + 4 * (1 - odd) * (1 - is_two))

    barrier = pltpu.get_barrier_semaphore()
    peers = [(g, x_peer), (mirror, me)]
    peers += [(g, at(o)) for o in (2, -2, 3, -3)]
    peers += [(g, at(4 * n)) for n in range(1, layers)]
    for peer in peers:
        pl.semaphore_signal(barrier, inc=1, device_id=peer, device_id_type=MESH)

    def own_slice(k):
        return ints_ref.at[:, pl.ds(pl.multiple_of(k * depth, depth), depth)]

    def load(k):
        return pltpu.make_async_copy(own_slice(k), buf.at[0, k], load_sem.at[k])

    def flow(lane, k, slot, to):
        return pltpu.make_async_remote_copy(
            src_ref=own_slice(k),
            dst_ref=buf.at[slot, k],
            send_sem=send_sem.at[lane, k],
            recv_sem=recv_sem.at[lane, k],
            device_id=(g, to),
            device_id_type=MESH,
        )

    def flow_col(k):
        return flow(0, k, 1, col_to)

    def flow_other(k):
        return flow(1, k, other_slot, other_to)

    def flow_down(k):
        return flow(2, k, 3, at(-4))

    def reflect(slot, k):
        return pltpu.make_async_remote_copy(
            src_ref=buf.at[slot, k],
            dst_ref=mir.at[slot, k],
            send_sem=mirror_send.at[slot, k],
            recv_sem=mirror_recv.at[slot, k],
            device_id=(mirror, me),
            device_id_type=MESH,
        )

    small = [
        pltpu.make_async_copy(source, target, small_sem.at[n])
        for n, (source, target) in enumerate(
            ((energy_in, energy_ref), (window_in, window_ref), (virt_in, virt_ref))
        )
    ]

    @pl.loop(0, slices)
    def _(k):
        load(k).start()

    for copy in small:
        copy.start()

    pl.semaphore_wait(barrier, len(peers))

    @pl.loop(0, slices)
    def _(k):
        flow_col(k).start()
        flow_other(k).start()

        @pl.when(place == 0)
        def _():
            flow_down(k).start()

    @pl.loop(0, slices)
    def _(k):
        load(k).wait()
        reflect(0, k).start()

    for copy in small:
        copy.wait()

    def virt_row(group, n):
        return virt_ref[pl.ds(group * parts + n, 1), :]

    for n in range(parts):
        mine, theirs = virt_row(g, n), virt_row(mirror, n)
        lanes = slice(n % 2 * 128, (n % 2 + 1) * 128)
        cols_virt[n // 2, :, lanes] = mine
        cols_virt[tiles + n // 2, :, lanes] = theirs
        rows_virt[n * 128 : (n + 1) * 128, :] = jnp.transpose(jnp.broadcast_to(mine, (128, 128)))

    def level(index):
        return energy_ref[window_ref[index]]

    own_level, col_level, b_level, r_level = level(me), level(col_id), level(b_id), level(r_id)

    def clear(pair):
        @pl.loop(0, 2 * tiles)
        def _(n):
            acc[pair, n] = jnp.zeros(acc.shape[2:], jnp.float32)

    def couple(pair, row_slot, k, cols, first_at):
        for n in range(tiles):
            side = cols[n * TILE : (n + 1) * TILE, :]
            for r in range(0, width, TILE):
                rows = slice(r, r + TILE)
                acc[pair, first_at + n, rows] += product(buf[row_slot, k, rows], side)

    def couple_near(pair, row_slot, col_slot, k):
        couple(pair, row_slot, k, buf.at[col_slot, k], 0)

    def couple_far(pair, row_slot, col_slot, k):
        couple(pair, row_slot, k, mir.at[col_slot, k], tiles)

    def amplitudes(pair, n, levels, energy_at, highs, lows):
        total = jnp.zeros((8, 128), jnp.float32)
        shifted_cols = [
            cols_virt[n, :, h * 128 : (h + 1) * 128] - levels for h in range(TILE // 128)
        ]
        for r in range(width // ROWS):
            span = slice(r * ROWS, (r + 1) * ROWS)
            base = rows_virt[span, :]
            for h in range(TILE // 128):
                lanes = slice(h * 128, (h + 1) * 128)
                coupling = acc[pair, n, span, lanes]
                amplitude = coupling / (base + shifted_cols[h])
                term = amplitude * coupling
                total = total + jnp.sum(term.reshape(ROWS // 8, 8, 128), axis=0)
                high = amplitude.astype(jnp.bfloat16)
                highs[span, lanes] = high
                lows[span, lanes] = (amplitude - high.astype(jnp.float32)).astype(jnp.bfloat16)
        evec[energy_at] += total

    def slabs_of(start, stop):
        for s in range(start // slab, -(-stop // slab)):
            low, high = max(start, s * slab), min(stop, (s + 1) * slab)
            yield (s // 4, (s // 2) % 2, s % 2), low, high, s * slab

    def densities(n, *splits, step=None):
        start, stop = n * TILE, (n + 1) * TILE
        step = step or TILE
        for first_row in range(0, stop, step):
            end_row = first_row + step
            update = None
            for highs, lows in splits:
                high, low = highs[first_row:end_row, :], lows[first_row:end_row, :]
                turn_high, turn_low = highs[start:stop, :], lows[start:stop, :]
                part = product(
                    jnp.concatenate([high, high, low], axis=1),
                    jnp.concatenate([turn_high, turn_low, turn_high], axis=1),
                )
                update = part if update is None else update + part
            for where, low_row, high_row, origin in slabs_of(first_row, end_row):
                dens[
                    (*where, slice(low_row - origin, high_row - origin), slice(start, stop))
                ] += update[low_row - first_row : high_row - first_row]

    evec[...] = jnp.zeros(evec.shape, jnp.float32)
    dens[...] = jnp.zeros(dens.shape, jnp.float32)

    clear(0)

    @pl.loop(0, slices)
    def _(k):
        couple_near(0, 0, 0, k)

    @pl.loop(0, slices)
    def _(k):
        reflect(0, k).wait_recv()
        couple_far(0, 0, 0, k)

    @pl.loop(0, 2 * tiles)
    def _(n):
        amplitudes(0, n, own_level + own_level, 0, split.at[0], split.at[1])
        for m in range(tiles):
            densities(m, (split.at[0], split.at[1]))

    for pair in range(3):
        clear(pair)

    @pl.loop(0, slices)
    def _(k):
        flow_col(k).wait_recv()
        reflect(1, k).start()
        flow_other(k).wait_recv()

        @pl.when(even)
        def _():
            reflect(2, k).start()

        @pl.when(place == 0)
        def _():
            flow_down(k).wait_recv()

        couple_near(0, b_slot, 1, k)
        couple_near(1, r_slot, b_slot, k)
        couple_near(2, r_slot, 1, k)
        reflect(1, k).wait_recv()

        @pl.when(even)
        def _():
            reflect(2, k).wait_recv()

        couple_far(0, b_slot, 1, k)
        couple_far(1, r_slot, b_slot, k)
        couple_far(2, r_slot, 1, k)

    @pl.loop(0, slices)
    def _(k):
        reflect(1, k).wait_send()

        @pl.when(even)
        def _():
            reflect(2, k).wait_send()

    def levels_of(pair):
        return jnp.where(
            pair == 0,
            b_level + col_level,
            jnp.where(pair == 1, r_level + b_level, r_level + col_level),
        )

    def kept(half, store):
        first_slot = store.shape[0] - 3
        slot, at_slice = half // (slices // 2), half % (slices // 2)
        return store.at[first_slot + slot, 2 * at_slice], store.at[first_slot + slot, 2 * at_slice + 1]

    def finish(t, highs, lows):
        pair, n = t // (2 * tiles), t % (2 * tiles)
        amplitudes(pair, n, levels_of(pair), 1 + pair, highs, lows)

    last = tiles - 1
    halves = 3 * tiles
    finish(0, *kept(0, mir))

    @pl.loop(0, halves - 1)
    def _(half):
        finish(2 * half + 1, *kept(half, buf))
        densities(last, kept(half, mir))
        finish(2 * half + 2, *kept(half + 1, mir))
        densities(last, kept(half, buf))

    finish(6 * tiles - 1, *kept(halves - 1, buf))
    densities(last, kept(halves - 1, mir))
    densities(last, kept(halves - 1, buf))

    def turn(n, m):
        block = [
            dens[(*where, slice(low - origin, high - origin), slice(m * TILE, (m + 1) * TILE))]
            for where, low, high, origin in slabs_of(n * TILE, (n + 1) * TILE)
        ]
        turned = jnp.transpose(jnp.concatenate(block, axis=0))
        for where, low, high, origin in slabs_of(m * TILE, (m + 1) * TILE):
            dens[(*where, slice(low - origin, high - origin), slice(n * TILE, (n + 1) * TILE))] = (
                turned[low - m * TILE : high - m * TILE]
            )

    def remote(source, target, sent, received, to):
        return pltpu.make_async_remote_copy(
            src_ref=source,
            dst_ref=target,
            send_sem=sent,
            recv_sem=received,
            device_id=to,
            device_id_type=MESH,
        )

    def lanes_of(n):
        return slice(n * 128, (n + 1) * 128)

    def first(n):
        if n % 2 == 0:
            source, to = dens.at[:, :, 1 - x_at, :, lanes_of(n)], x_peer
        else:
            source, to = dens.at[:, 1 - y_at, :, :, lanes_of(n)], y_peer
        return remote(source, first_in.at[n], first_send.at[n], first_recv.at[n], (g, to))

    def second(n):
        if n % 2 == 0:
            source, to = dens.at[:, 1 - y_at, x_at, :, lanes_of(n)], y_peer
        else:
            source, to = dens.at[:, y_at, 1 - x_at, :, lanes_of(n)], x_peer
        return remote(source, second_in.at[n], second_send.at[n], second_recv.at[n], (g, to))

    def third(n, step):
        to = at(4 * step)
        return remote(
            dens.at[to // 4, y_at, x_at, :, lanes_of(n)],
            third_in.at[n, step - 1],
            third_send.at[n, step - 1],
            third_recv.at[n, step - 1],
            (g, to),
        )

    for n in (2 * last, 2 * last + 1):
        first(n).start()

    share = remote(evec, ein, energy_send.at[0], energy_recv.at[0], (mirror, me))
    share.start()
    for m in range(last):
        turn(m, last)
    to_b = remote(etot.at[1], eback, energy_send.at[1], energy_recv.at[1], (g, y_peer))
    to_r = remote(etot.at[pl.ds(2, 2)], efar, energy_send.at[2], energy_recv.at[2], (g, r_id))

    def take_first(n):
        first(n).wait_recv()
        if n % 2 == 0:
            dens[:, :, x_at, :, lanes_of(n)] += first_in[n]
        else:
            dens[:, y_at, :, :, lanes_of(n)] += first_in[n]
        second(n).start()

    def take_second(n):
        second(n).wait_recv()
        dens[:, y_at, x_at, :, lanes_of(n)] += second_in[n]
        for step in range(1, layers):
            third(n, step).start()

    waiting = [2 * last, 2 * last + 1]
    halfway = []
    for n in range(last - 1, -1, -1):

        @pl.loop(0, 3)
        def _(third_of):
            densities(
                n,
                *(
                    kept(third_of * tiles + step, store)
                    for step in range(tiles)
                    for store in (mir, buf)
                ),
            )

        for m in (2 * n, 2 * n + 1):
            first(m).start()
        for m in range(n):
            turn(m, n)
        if n == last - 1:
            share.wait()
            etot[...] = evec[...] + ein[...]

            @pl.when(even)
            def _():
                to_b.start()

            @pl.when(is_two == 0)
            def _():
                to_r.start()

        for m in waiting:
            take_first(m)
        for m in halfway:
            take_second(m)
        waiting, halfway = [2 * n, 2 * n + 1], waiting
    for m in waiting:
        take_first(m)
    for m in halfway + waiting:
        take_second(m)

    efin[...] = etot[...]

    @pl.when(even)
    def _():
        to_b.wait()
        efin[1] = eback[...]

    @pl.when(is_two == 0)
    def _():
        to_r.wait()
        efin[2:4] = efar[...]

    lane = lax.broadcasted_iota(jnp.int32, (1, 4), 1)
    energies = jnp.zeros((1, 4), jnp.float32)
    for s in range(4):
        energies = jnp.where(lane == s, -jnp.sum(efin[s]) / (width * width), energies)
    pairs_ref[...] = energies

    for n in range(parts):
        value = dens[z_at, y_at, x_at, :, lanes_of(n)]
        for step in range(1, layers):
            third(n, step).wait_recv()
            value = value + third_in[n, step - 1]
        density_ref[:, lanes_of(n)] = value / (count * STEPS)

    for n in range(parts):
        first(n).wait_send()
        second(n).wait_send()
        for step in range(1, layers):
            third(n, step).wait_send()

    @pl.loop(0, slices)
    def _(k):
        flow_col(k).wait_send()
        flow_other(k).wait_send()
        reflect(0, k).wait_send()

        @pl.when(place == 0)
        def _():
            flow_down(k).wait_send()


def fused(count, ints, occ_energy, occ_window, virt_energy):
    width, depth = ints.shape[1:]
    slices, layers, slab = depth // SLICE, count // 4, width // count
    tiles, parts = width // TILE, width // 128
    dma = pltpu.SemaphoreType.DMA
    return pl.pallas_call(
        functools.partial(fused_kernel, count),
        out_shape=(
            jax.ShapeDtypeStruct((slab, width), jnp.float32),
            jax.ShapeDtypeStruct((1, STEPS), jnp.float32),
        ),
        in_specs=[
            pl.BlockSpec(memory_space=pl.ANY),
            pl.BlockSpec(memory_space=pl.ANY),
            pl.BlockSpec(memory_space=pl.ANY),
            pl.BlockSpec(memory_space=pl.ANY),
        ],
        out_specs=(
            pl.BlockSpec(memory_space=pltpu.VMEM),
            pl.BlockSpec(memory_space=pltpu.VMEM),
        ),
        scratch_shapes=[
            pltpu.SMEM(occ_energy.shape, jnp.float32),
            pltpu.SMEM(occ_window.shape, jnp.int32),
            pltpu.VMEM((virt_energy.shape[0] // 128, 128), jnp.float32),
            pltpu.VMEM((4, slices, width, SLICE), jnp.bfloat16),
            pltpu.VMEM((3, slices, width, SLICE), jnp.bfloat16),
            pltpu.VMEM((3, 2 * tiles, width, TILE), jnp.float32),
            pltpu.VMEM((layers, 2, 2, slab, width), jnp.float32),
            pltpu.VMEM((2, width, TILE), jnp.bfloat16),
            pltpu.VMEM((width, 128), jnp.float32),
            pltpu.VMEM((2 * tiles, 1, TILE), jnp.float32),
            pltpu.VMEM((parts, layers, 2, slab, 128), jnp.float32),
            pltpu.VMEM((parts, layers, slab, 128), jnp.float32),
            pltpu.VMEM((parts, layers - 1, slab, 128), jnp.float32),
            pltpu.VMEM((4, 8, 128), jnp.float32),
            pltpu.VMEM((4, 8, 128), jnp.float32),
            pltpu.VMEM((4, 8, 128), jnp.float32),
            pltpu.VMEM((8, 128), jnp.float32),
            pltpu.VMEM((2, 8, 128), jnp.float32),
            pltpu.VMEM((4, 8, 128), jnp.float32),
            dma((3,)),
            dma((slices,)),
            dma((3, slices)),
            dma((3, slices)),
            dma((3, slices)),
            dma((3, slices)),
            dma((parts,)),
            dma((parts,)),
            dma((parts,)),
            dma((parts,)),
            dma((parts, layers - 1)),
            dma((parts, layers - 1)),
            dma((3,)),
            dma((3,)),
        ],
        compiler_params=pltpu.CompilerParams(
            collective_id=0, has_side_effects=True, vmem_limit_bytes=67043328
        ),
    )(ints[0], occ_energy, occ_window, virt_energy.reshape(-1, 128))


def fused_or_local(mesh, ints, occ_energy, occ_window, virt_energy):
    groups, blocks = mesh.shape["grp"], mesh.shape["blk"]
    occ_dev, width, depth = ints.shape
    fits = occ_dev == 1 and STEPS == 4 and groups % 2 == 0 and blocks % 4 == 0 and blocks >= 8
    fits = fits and width % TILE == 0 and width % (8 * blocks) == 0 and depth % SLICE == 0
    fits = fits and width > TILE and depth // SLICE >= 4 * (width // TILE)
    if fits:
        return fused(blocks, ints, occ_energy, occ_window, virt_energy)
    return local(ints, occ_energy, occ_window, virt_energy)


def solution(mesh):
    return jax.shard_map(
        functools.partial(fused_or_local, mesh),
        mesh=mesh,
        in_specs=(P("blk", "grp", None), P(), P(), P()),
        out_specs=(P(("grp", "blk"), None), P("blk", None)),
        check_vma=False,
    )
```

```python
import functools

import jax
import jax.numpy as jnp
from jax import lax
from jax.experimental import pallas as pl
from jax.experimental.pallas import tpu as pltpu
from jax.sharding import PartitionSpec as P

STEPS = 4
CHUNKS = 1
RELAY = False


def from_partner(block, axis, stride):
    count = lax.axis_size(axis)
    route = []
    for low in range(count):
        high = low | 1 << stride
        if high != low and high < count:
            route += [(low, high), (high, low)]
    return lax.ppermute(block, axis, route)


def shifted(shard, axis, by):
    peers = lax.axis_size(axis)
    return lax.ppermute(shard, axis, [(i, (i + by) % peers) for i in range(peers)])


def lookup_many(values_in, where_at):
    positions = jnp.arange(values_in.shape[0], dtype=jnp.int32)
    matches = positions[None, :] == where_at[:, None]
    return jnp.sum(
        jnp.where(matches, values_in[None, :], jnp.zeros_like(values_in)[None, :]), axis=1
    )


def fetched(pieces, block_index, block_count):
    if not RELAY or block_count % 4:
        return (
            [shifted(piece, "blk", -2) for piece in pieces],
            [shifted(piece, "blk", 1) for piece in pieces],
        )
    blocks = range(block_count)
    cross_y = [(c, c ^ 2) for c in blocks]
    down = [(c, (c - 4) % block_count) for c in blocks if c & 2]
    evens = [(c, c + 1) for c in blocks if c % 2 == 0]
    odds = [(c, (c + (-1 if c & 2 else 3)) % block_count) for c in blocks if c % 2]
    upper = (block_index & 2) != 0
    odd = (block_index & 1) != 0
    further, back = [], []
    for piece in pieces:
        over = lax.ppermute(piece, "blk", cross_y)
        direct = lax.ppermute(piece, "blk", evens)
        relayed = lax.ppermute(over, "blk", odds)
        further.append(jnp.where(upper, lax.ppermute(over, "blk", down), over))
        back.append(jnp.where(odd, direct, relayed))
    return further, back


def local(ints, occ_energy, occ_window, virt_energy):
    occ_dev = ints.shape[0]
    virt_width = ints.shape[1]
    occ_count = occ_window.shape[0]
    block_count = occ_count // occ_dev
    group_index = lax.axis_index("grp")
    block_index = lax.axis_index("blk")
    mirror_index = group_index + 1 - 2 * (group_index % 2)
    virt_own = lax.dynamic_slice_in_dim(virt_energy, group_index * virt_width, virt_width)
    virt_mirror = lax.dynamic_slice_in_dim(virt_energy, mirror_index * virt_width, virt_width)
    local_rows = jnp.arange(occ_dev, dtype=jnp.int32)

    def levels(offset):
        block = (block_index + offset) % block_count
        return lookup_many(occ_energy, lookup_many(occ_window, block * occ_dev + local_rows))

    occ_own, occ_back, occ_further = levels(0), levels(-1), levels(2)
    chunks = CHUNKS if virt_width % (16 * CHUNKS) == 0 else 1
    size = virt_width // chunks
    pieces = [ints[:, n * size : (n + 1) * size] for n in range(chunks)]
    mirror = from_partner(ints, "grp", 0)
    further_pieces, back_pieces = fetched(pieces, block_index, block_count)
    virt_pieces = [
        (virt_own[n * size : (n + 1) * size], virt_mirror[n * size : (n + 1) * size])
        for n in range(chunks)
    ]

    def tile(rows, cols, virt_cols, occ_rows, occ_cols):
        coupling = jnp.einsum("rap,tbp->rtab", rows, cols, preferred_element_type=jnp.float32)
        denominator = (
            virt_own[None, None, :, None]
            + virt_cols[None, None, None, :]
            - occ_rows[:, None, None, None]
            - occ_cols[None, :, None, None]
        )
        amplitude = coupling / denominator
        square = amplitude * amplitude
        energy = -jnp.sum(square * denominator, axis=(2, 3)) / (virt_width * virt_width)
        kept = lax.reduce_precision(amplitude, exponent_bits=8, mantissa_bits=7)
        high = kept.astype(jnp.bfloat16)
        low = (amplitude - kept).astype(jnp.bfloat16)
        main = jnp.einsum("rtab,rtcb->ac", high, high, preferred_element_type=jnp.float32)
        side = jnp.einsum("rtab,rtcb->ac", high, low, preferred_element_type=jnp.float32)
        return main, side, energy

    def add(one, other):
        return tuple(a + b for a, b in zip(one, other))

    zero = add(
        tile(ints, ints, virt_own, occ_own, occ_own),
        tile(ints, mirror, virt_mirror, occ_own, occ_own),
    )
    one = None
    for piece, (near, far) in zip(back_pieces, virt_pieces):
        part = add(
            tile(ints, piece, near, occ_own, occ_back),
            tile(ints, from_partner(piece, "grp", 0), far, occ_own, occ_back),
        )
        one = part if one is None else add(one, part)
    further = jnp.concatenate(further_pieces, axis=1)
    two = add(
        tile(further, ints, virt_own, occ_further, occ_own),
        tile(further, mirror, virt_mirror, occ_further, occ_own),
    )
    three = None
    for piece, (near, far) in zip(back_pieces, virt_pieces):
        part = add(
            tile(further, piece, near, occ_further, occ_back),
            tile(further, from_partner(piece, "grp", 0), far, occ_further, occ_back),
        )
        three = part if three is None else add(three, part)
    main, side = add(add(zero[:2], one[:2]), add(two[:2], three[:2]))
    density = main + side + side.T
    shares = lax.psum_scatter(density, "blk", scatter_dimension=0, tiled=True) / (
        occ_count * STEPS * occ_dev
    )
    sent = shifted(jnp.concatenate([two[2], three[2]], axis=1), "blk", 2)
    energies = jnp.concatenate([zero[2], one[2], sent], axis=1)
    return (shares, energies + from_partner(energies, "grp", 0))


MESH = pl.DeviceIdType.MESH
TILE = 256
SLICE = 256
ROWS = 64
LATE = 2
NT = (((1,), (1,)), ((), ()))


def product(rows, cols):
    return lax.dot_general(rows, cols, NT, preferred_element_type=jnp.float32)


def fused_kernel(
    count,
    ints_ref,
    energy_in,
    window_in,
    virt_in,
    density_ref,
    pairs_ref,
    energy_ref,
    window_ref,
    virt_ref,
    buf,
    mir,
    acc,
    dens,
    split,
    rows_virt,
    cols_virt,
    first_in,
    second_in,
    third_in,
    across_in,
    evec,
    ein,
    etot,
    eback,
    efar,
    efin,
    small_sem,
    load_sem,
    send_sem,
    recv_sem,
    mirror_send,
    mirror_recv,
    first_send,
    first_recv,
    second_send,
    second_recv,
    third_send,
    third_recv,
    energy_send,
    energy_recv,
):
    g = lax.axis_index("grp")
    me = lax.axis_index("blk")
    slices, width, depth = buf.shape[1:]
    layers = count // 4
    slab = dens.shape[3]
    tiles = width // TILE
    parts = width // 128
    place = me % 4
    x_at, y_at, z_at = me % 2, (me // 2) % 2, me // 4
    odd = place % 2
    even = odd == 0
    mirror = g + 1 - 2 * (g % 2)

    def at(offset):
        return (me + offset + count) % count

    x_peer = me + 1 - 2 * x_at
    y_peer = me + 2 - 4 * y_at
    is_two = (place // 2) * (1 - odd)
    col_to = at(1 - 2 * odd + 4 * (place // 3))
    other_to = at(2 - 4 * ((place + 3) // 4))
    other_slot = 2 + odd
    b_slot = 2 * (1 - odd)
    r_slot = 3 - 3 * is_two
    col_id = at(1 - 2 * ((place + 3) // 4) - 2 * is_two)
    b_id = at((1 - odd) * (2 - 4 * is_two))
    r_id = at(2 * odd + 4 * (1 - odd) * (1 - is_two))

    barrier = pltpu.get_barrier_semaphore()
    peers = [(g, x_peer), (mirror, me)]
    peers += [(g, at(o)) for o in (2, -2, 3, -3)]
    peers += [(g, at(4 * n)) for n in range(1, layers)]
    for peer in peers:
        pl.semaphore_signal(barrier, inc=1, device_id=peer, device_id_type=MESH)

    def load(k):
        return pltpu.make_async_copy(
            ints_ref.at[:, pl.ds(pl.multiple_of(k * depth, depth), depth)],
            buf.at[0, k],
            load_sem.at[k],
        )

    def flow(lane, k, slot, to):
        return pltpu.make_async_remote_copy(
            src_ref=buf.at[0, k],
            dst_ref=buf.at[slot, k],
            send_sem=send_sem.at[lane, k],
            recv_sem=recv_sem.at[lane, k],
            device_id=(g, to),
            device_id_type=MESH,
        )

    def flow_col(k):
        return flow(0, k, 1, col_to)

    def flow_other(k):
        return flow(1, k, other_slot, other_to)

    def flow_down(k):
        return flow(2, k, 3, at(-4))

    def reflect(slot, k):
        return pltpu.make_async_remote_copy(
            src_ref=buf.at[slot, k],
            dst_ref=mir.at[slot, k],
            send_sem=mirror_send.at[slot, k],
            recv_sem=mirror_recv.at[slot, k],
            device_id=(mirror, me),
            device_id_type=MESH,
        )

    small = [
        pltpu.make_async_copy(source, target, small_sem.at[n])
        for n, (source, target) in enumerate(
            ((energy_in, energy_ref), (window_in, window_ref), (virt_in, virt_ref))
        )
    ]

    @pl.loop(0, slices)
    def _(k):
        load(k).start()

    for copy in small:
        copy.start()

    pl.semaphore_wait(barrier, len(peers))

    @pl.loop(0, slices)
    def _(k):
        load(k).wait()
        flow_col(k).start()
        flow_other(k).start()

        @pl.when(place == 0)
        def _():
            flow_down(k).start()

        reflect(0, k).start()

    for copy in small:
        copy.wait()

    def virt_row(group, n):
        return virt_ref[pl.ds(group * parts + n, 1), :]

    for n in range(parts):
        mine, theirs = virt_row(g, n), virt_row(mirror, n)
        lanes = slice(n % 2 * 128, (n % 2 + 1) * 128)
        cols_virt[n // 2, :, lanes] = mine
        cols_virt[tiles + n // 2, :, lanes] = theirs
        rows_virt[n * 128 : (n + 1) * 128, :] = jnp.transpose(jnp.broadcast_to(mine, (128, 128)))

    def level(index):
        return energy_ref[window_ref[index]]

    own_level, col_level, b_level, r_level = level(me), level(col_id), level(b_id), level(r_id)

    def clear(pair):
        @pl.loop(0, 2 * tiles)
        def _(n):
            acc[pair, n] = jnp.zeros(acc.shape[2:], jnp.float32)

    def couple(pair, row_slot, k, cols, first_at):
        for n in range(tiles):
            side = cols[n * TILE : (n + 1) * TILE, :]
            for r in range(0, width, TILE):
                rows = slice(r, r + TILE)
                acc[pair, first_at + n, rows] += product(buf[row_slot, k, rows], side)

    def couple_near(pair, row_slot, col_slot, k):
        couple(pair, row_slot, k, buf.at[col_slot, k], 0)

    def couple_far(pair, row_slot, col_slot, k):
        couple(pair, row_slot, k, mir.at[col_slot, k], tiles)

    def amplitudes(pair, n, levels, energy_at, highs, lows):
        total = jnp.zeros((8, 128), jnp.float32)
        shifted_cols = [
            cols_virt[n, :, h * 128 : (h + 1) * 128] - levels for h in range(TILE // 128)
        ]
        for r in range(width // ROWS):
            span = slice(r * ROWS, (r + 1) * ROWS)
            base = rows_virt[span, :]
            for h in range(TILE // 128):
                lanes = slice(h * 128, (h + 1) * 128)
                coupling = acc[pair, n, span, lanes]
                amplitude = coupling / (base + shifted_cols[h])
                term = amplitude * coupling
                total = total + jnp.sum(term.reshape(ROWS // 8, 8, 128), axis=0)
                high = amplitude.astype(jnp.bfloat16)
                highs[span, lanes] = high
                lows[span, lanes] = (amplitude - high.astype(jnp.float32)).astype(jnp.bfloat16)
        evec[energy_at] += total

    def slabs_of(start, stop):
        for s in range(start // slab, -(-stop // slab)):
            low, high = max(start, s * slab), min(stop, (s + 1) * slab)
            yield (s // 4, (s // 2) % 2, s % 2), low, high, s * slab

    def densities(n, *splits, step=None):
        start, stop = n * TILE, (n + 1) * TILE
        step = step or TILE
        for first_row in range(0, stop, step):
            end_row = first_row + step
            update = None
            for highs, lows in splits:
                high, low = highs[first_row:end_row, :], lows[first_row:end_row, :]
                turn_high, turn_low = highs[start:stop, :], lows[start:stop, :]
                part = product(
                    jnp.concatenate([high, high, low], axis=1),
                    jnp.concatenate([turn_high, turn_low, turn_high], axis=1),
                )
                update = part if update is None else update + part
            for where, low_row, high_row, origin in slabs_of(first_row, end_row):
                dens[
                    (*where, slice(low_row - origin, high_row - origin), slice(start, stop))
                ] += update[low_row - first_row : high_row - first_row]

    evec[...] = jnp.zeros(evec.shape, jnp.float32)
    dens[...] = jnp.zeros(dens.shape, jnp.float32)

    clear(0)

    @pl.loop(0, slices)
    def _(k):
        couple_near(0, 0, 0, k)

    @pl.loop(0, slices)
    def _(k):
        reflect(0, k).wait_recv()
        couple_far(0, 0, 0, k)

    @pl.loop(0, 2 * tiles)
    def _(n):
        amplitudes(0, n, own_level + own_level, 0, split.at[0], split.at[1])
        for m in range(tiles):
            densities(m, (split.at[0], split.at[1]))

    for pair in range(3):
        clear(pair)

    @pl.loop(0, slices)
    def _(k):
        flow_col(k).wait_recv()
        reflect(1, k).start()
        flow_other(k).wait_recv()

        @pl.when(even)
        def _():
            reflect(2, k).start()

        @pl.when(place == 0)
        def _():
            flow_down(k).wait_recv()

        couple_near(0, b_slot, 1, k)
        couple_near(1, r_slot, b_slot, k)
        couple_near(2, r_slot, 1, k)
        reflect(1, k).wait_recv()

        @pl.when(even)
        def _():
            reflect(2, k).wait_recv()

        couple_far(0, b_slot, 1, k)
        couple_far(1, r_slot, b_slot, k)
        couple_far(2, r_slot, 1, k)

    @pl.loop(0, slices)
    def _(k):
        reflect(1, k).wait_send()

        @pl.when(even)
        def _():
            reflect(2, k).wait_send()

    def levels_of(pair):
        return jnp.where(
            pair == 0,
            b_level + col_level,
            jnp.where(pair == 1, r_level + b_level, r_level + col_level),
        )

    def kept(half, store):
        first_slot = store.shape[0] - 3
        slot, at_slice = half // (slices // 2), half % (slices // 2)
        return store.at[first_slot + slot, 2 * at_slice], store.at[first_slot + slot, 2 * at_slice + 1]

    def finish(t, highs, lows):
        pair, n = t // (2 * tiles), t % (2 * tiles)
        amplitudes(pair, n, levels_of(pair), 1 + pair, highs, lows)

    last = tiles - 1
    halves = 3 * tiles
    finish(0, *kept(0, mir))

    @pl.loop(0, halves - 1)
    def _(half):
        finish(2 * half + 1, *kept(half, buf))
        densities(last, kept(half, mir))
        finish(2 * half + 2, *kept(half + 1, mir))
        densities(last, kept(half, buf))

    finish(6 * tiles - 1, *kept(halves - 1, buf))
    densities(last, kept(halves - 1, mir))
    densities(last, kept(halves - 1, buf))

    def turn(n, m):
        block = [
            dens[(*where, slice(low - origin, high - origin), slice(m * TILE, (m + 1) * TILE))]
            for where, low, high, origin in slabs_of(n * TILE, (n + 1) * TILE)
        ]
        turned = jnp.transpose(jnp.concatenate(block, axis=0))
        for where, low, high, origin in slabs_of(m * TILE, (m + 1) * TILE):
            dens[(*where, slice(low - origin, high - origin), slice(n * TILE, (n + 1) * TILE))] = (
                turned[low - m * TILE : high - m * TILE]
            )

    def remote(source, target, sent, received, to):
        return pltpu.make_async_remote_copy(
            src_ref=source,
            dst_ref=target,
            send_sem=sent,
            recv_sem=received,
            device_id=to,
            device_id_type=MESH,
        )

    def lanes_of(n):
        return slice(n * 128, (n + 1) * 128)

    def first(n):
        if n % 2 == 0:
            source, to = dens.at[:, :, 1 - x_at, :, lanes_of(n)], x_peer
        else:
            source, to = dens.at[:, 1 - y_at, :, :, lanes_of(n)], y_peer
        return remote(source, first_in.at[n], first_send.at[n], first_recv.at[n], (g, to))

    def second(n):
        if n % 2 == 0:
            source, to = dens.at[:, 1 - y_at, x_at, :, lanes_of(n)], y_peer
        else:
            source, to = dens.at[:, y_at, 1 - x_at, :, lanes_of(n)], x_peer
        return remote(source, second_in.at[n], second_send.at[n], second_recv.at[n], (g, to))

    def third(n, step):
        to = at(4 * step)
        return remote(
            dens.at[to // 4, y_at, x_at, :, lanes_of(n)],
            third_in.at[n, step - 1],
            third_send.at[n, step - 1],
            third_recv.at[n, step - 1],
            (g, to),
        )

    def across(n, step):
        to = at(4 * step)
        if n % 2 == 0:
            source = dens.at[to // 4, :, x_at, :, lanes_of(n)]
        else:
            source = dens.at[to // 4, y_at, :, :, lanes_of(n)]
        return remote(
            source,
            across_in.at[n, step - 1],
            third_send.at[n, step - 1],
            third_recv.at[n, step - 1],
            (g, to),
        )

    def closing(n):
        if n % 2 == 0:
            source, to = dens.at[z_at, 1 - y_at, x_at, :, lanes_of(n)], y_peer
        else:
            source, to = dens.at[z_at, y_at, 1 - x_at, :, lanes_of(n)], x_peer
        return remote(source, second_in.at[n, 0], second_send.at[n], second_recv.at[n], (g, to))

    for n in (2 * last, 2 * last + 1):
        first(n).start()

    share = remote(evec, ein, energy_send.at[0], energy_recv.at[0], (mirror, me))
    share.start()
    for m in range(last):
        turn(m, last)
    to_b = remote(etot.at[1], eback, energy_send.at[1], energy_recv.at[1], (g, y_peer))
    to_r = remote(etot.at[pl.ds(2, 2)], efar, energy_send.at[2], energy_recv.at[2], (g, r_id))

    def take_first(n):
        first(n).wait_recv()
        if n % 2 == 0:
            dens[:, :, x_at, :, lanes_of(n)] += first_in[n]
        else:
            dens[:, y_at, :, :, lanes_of(n)] += first_in[n]
        if n >= LATE:
            second(n).start()
            return
        for step in range(1, layers):
            across(n, step).start()

    def take_second(n):
        if n < LATE:
            for step in range(1, layers):
                across(n, step).wait_recv()
                if n % 2 == 0:
                    dens[z_at, :, x_at, :, lanes_of(n)] += across_in[n, step - 1]
                else:
                    dens[z_at, y_at, :, :, lanes_of(n)] += across_in[n, step - 1]
            closing(n).start()
            return
        second(n).wait_recv()
        dens[:, y_at, x_at, :, lanes_of(n)] += second_in[n]
        for step in range(1, layers):
            third(n, step).start()

    waiting = [2 * last, 2 * last + 1]
    halfway = []
    for n in range(last - 1, -1, -1):

        @pl.loop(0, 3)
        def _(third_of):
            densities(
                n,
                *(
                    kept(third_of * tiles + step, store)
                    for step in range(tiles)
                    for store in (mir, buf)
                ),
            )

        for m in (2 * n, 2 * n + 1):
            first(m).start()
        for m in range(n):
            turn(m, n)
        if n == last - 1:
            share.wait()
            etot[...] = evec[...] + ein[...]

            @pl.when(even)
            def _():
                to_b.start()

            @pl.when(is_two == 0)
            def _():
                to_r.start()

        for m in waiting:
            take_first(m)
        for m in halfway:
            take_second(m)
        waiting, halfway = [2 * n, 2 * n + 1], waiting
    for m in waiting:
        take_first(m)
    for m in halfway + waiting:
        take_second(m)

    efin[...] = etot[...]

    @pl.when(even)
    def _():
        to_b.wait()
        efin[1] = eback[...]

    @pl.when(is_two == 0)
    def _():
        to_r.wait()
        efin[2:4] = efar[...]

    lane = lax.broadcasted_iota(jnp.int32, (1, 4), 1)
    energies = jnp.zeros((1, 4), jnp.float32)
    for s in range(4):
        energies = jnp.where(lane == s, -jnp.sum(efin[s]) / (width * width), energies)
    pairs_ref[...] = energies

    for n in range(parts):
        value = dens[z_at, y_at, x_at, :, lanes_of(n)]
        if n < LATE:
            closing(n).wait_recv()
            value = value + second_in[n, 0]
        for step in range(1, layers if n >= LATE else 1):
            third(n, step).wait_recv()
            value = value + third_in[n, step - 1]
        density_ref[:, lanes_of(n)] = value / (count * STEPS)

    for n in range(parts):
        first(n).wait_send()
        (second if n >= LATE else closing)(n).wait_send()
        for step in range(1, layers):
            (third if n >= LATE else across)(n, step).wait_send()

    @pl.loop(0, slices)
    def _(k):
        flow_col(k).wait_send()
        flow_other(k).wait_send()
        reflect(0, k).wait_send()

        @pl.when(place == 0)
        def _():
            flow_down(k).wait_send()


def fused(count, ints, occ_energy, occ_window, virt_energy):
    width, depth = ints.shape[1:]
    slices, layers, slab = depth // SLICE, count // 4, width // count
    tiles, parts = width // TILE, width // 128
    dma = pltpu.SemaphoreType.DMA
    return pl.pallas_call(
        functools.partial(fused_kernel, count),
        out_shape=(
            jax.ShapeDtypeStruct((slab, width), jnp.float32),
            jax.ShapeDtypeStruct((1, STEPS), jnp.float32),
        ),
        in_specs=[
            pl.BlockSpec(memory_space=pl.ANY),
            pl.BlockSpec(memory_space=pl.ANY),
            pl.BlockSpec(memory_space=pl.ANY),
            pl.BlockSpec(memory_space=pl.ANY),
        ],
        out_specs=(
            pl.BlockSpec(memory_space=pltpu.VMEM),
            pl.BlockSpec(memory_space=pltpu.VMEM),
        ),
        scratch_shapes=[
            pltpu.SMEM(occ_energy.shape, jnp.float32),
            pltpu.SMEM(occ_window.shape, jnp.int32),
            pltpu.VMEM((virt_energy.shape[0] // 128, 128), jnp.float32),
            pltpu.VMEM((4, slices, width, SLICE), jnp.bfloat16),
            pltpu.VMEM((3, slices, width, SLICE), jnp.bfloat16),
            pltpu.VMEM((3, 2 * tiles, width, TILE), jnp.float32),
            pltpu.VMEM((layers, 2, 2, slab, width), jnp.float32),
            pltpu.VMEM((2, width, TILE), jnp.bfloat16),
            pltpu.VMEM((width, 128), jnp.float32),
            pltpu.VMEM((2 * tiles, 1, TILE), jnp.float32),
            pltpu.VMEM((parts, layers, 2, slab, 128), jnp.float32),
            pltpu.VMEM((parts, layers, slab, 128), jnp.float32),
            pltpu.VMEM((parts, layers - 1, slab, 128), jnp.float32),
            pltpu.VMEM((LATE, layers - 1, 2, slab, 128), jnp.float32),
            pltpu.VMEM((4, 8, 128), jnp.float32),
            pltpu.VMEM((4, 8, 128), jnp.float32),
            pltpu.VMEM((4, 8, 128), jnp.float32),
            pltpu.VMEM((8, 128), jnp.float32),
            pltpu.VMEM((2, 8, 128), jnp.float32),
            pltpu.VMEM((4, 8, 128), jnp.float32),
            dma((3,)),
            dma((slices,)),
            dma((3, slices)),
            dma((3, slices)),
            dma((3, slices)),
            dma((3, slices)),
            dma((parts,)),
            dma((parts,)),
            dma((parts,)),
            dma((parts,)),
            dma((parts, layers - 1)),
            dma((parts, layers - 1)),
            dma((3,)),
            dma((3,)),
        ],
        compiler_params=pltpu.CompilerParams(
            collective_id=0, has_side_effects=True, vmem_limit_bytes=67043328
        ),
    )(ints[0], occ_energy, occ_window, virt_energy.reshape(-1, 128))


def fused_or_local(mesh, ints, occ_energy, occ_window, virt_energy):
    groups, blocks = mesh.shape["grp"], mesh.shape["blk"]
    occ_dev, width, depth = ints.shape
    fits = occ_dev == 1 and STEPS == 4 and groups % 2 == 0 and blocks % 4 == 0 and blocks >= 8
    fits = fits and width % TILE == 0 and width % (8 * blocks) == 0 and depth % SLICE == 0
    fits = fits and width > TILE and depth // SLICE >= 4 * (width // TILE)
    if fits:
        return fused(blocks, ints, occ_energy, occ_window, virt_energy)
    return local(ints, occ_energy, occ_window, virt_energy)


def solution(mesh):
    return jax.shard_map(
        functools.partial(fused_or_local, mesh),
        mesh=mesh,
        in_specs=(P("blk", "grp", None), P(), P(), P()),
        out_specs=(P(("grp", "blk"), None), P("blk", None)),
        check_vma=False,
    )
```

```python
import functools

import jax
import jax.numpy as jnp
from jax import lax
from jax.experimental import pallas as pl
from jax.experimental.pallas import tpu as pltpu
from jax.sharding import PartitionSpec as P

STEPS = 4
CHUNKS = 1
RELAY = False


def from_partner(block, axis, stride):
    count = lax.axis_size(axis)
    route = []
    for low in range(count):
        high = low | 1 << stride
        if high != low and high < count:
            route += [(low, high), (high, low)]
    return lax.ppermute(block, axis, route)


def shifted(shard, axis, by):
    peers = lax.axis_size(axis)
    return lax.ppermute(shard, axis, [(i, (i + by) % peers) for i in range(peers)])


def lookup_many(values_in, where_at):
    positions = jnp.arange(values_in.shape[0], dtype=jnp.int32)
    matches = positions[None, :] == where_at[:, None]
    return jnp.sum(
        jnp.where(matches, values_in[None, :], jnp.zeros_like(values_in)[None, :]), axis=1
    )


def fetched(pieces, block_index, block_count):
    if not RELAY or block_count % 4:
        return (
            [shifted(piece, "blk", -2) for piece in pieces],
            [shifted(piece, "blk", 1) for piece in pieces],
        )
    blocks = range(block_count)
    cross_y = [(c, c ^ 2) for c in blocks]
    down = [(c, (c - 4) % block_count) for c in blocks if c & 2]
    evens = [(c, c + 1) for c in blocks if c % 2 == 0]
    odds = [(c, (c + (-1 if c & 2 else 3)) % block_count) for c in blocks if c % 2]
    upper = (block_index & 2) != 0
    odd = (block_index & 1) != 0
    further, back = [], []
    for piece in pieces:
        over = lax.ppermute(piece, "blk", cross_y)
        direct = lax.ppermute(piece, "blk", evens)
        relayed = lax.ppermute(over, "blk", odds)
        further.append(jnp.where(upper, lax.ppermute(over, "blk", down), over))
        back.append(jnp.where(odd, direct, relayed))
    return further, back


def local(ints, occ_energy, occ_window, virt_energy):
    occ_dev = ints.shape[0]
    virt_width = ints.shape[1]
    occ_count = occ_window.shape[0]
    block_count = occ_count // occ_dev
    group_index = lax.axis_index("grp")
    block_index = lax.axis_index("blk")
    mirror_index = group_index + 1 - 2 * (group_index % 2)
    virt_own = lax.dynamic_slice_in_dim(virt_energy, group_index * virt_width, virt_width)
    virt_mirror = lax.dynamic_slice_in_dim(virt_energy, mirror_index * virt_width, virt_width)
    local_rows = jnp.arange(occ_dev, dtype=jnp.int32)

    def levels(offset):
        block = (block_index + offset) % block_count
        return lookup_many(occ_energy, lookup_many(occ_window, block * occ_dev + local_rows))

    occ_own, occ_back, occ_further = levels(0), levels(-1), levels(2)
    chunks = CHUNKS if virt_width % (16 * CHUNKS) == 0 else 1
    size = virt_width // chunks
    pieces = [ints[:, n * size : (n + 1) * size] for n in range(chunks)]
    mirror = from_partner(ints, "grp", 0)
    further_pieces, back_pieces = fetched(pieces, block_index, block_count)
    virt_pieces = [
        (virt_own[n * size : (n + 1) * size], virt_mirror[n * size : (n + 1) * size])
        for n in range(chunks)
    ]

    def tile(rows, cols, virt_cols, occ_rows, occ_cols):
        coupling = jnp.einsum("rap,tbp->rtab", rows, cols, preferred_element_type=jnp.float32)
        denominator = (
            virt_own[None, None, :, None]
            + virt_cols[None, None, None, :]
            - occ_rows[:, None, None, None]
            - occ_cols[None, :, None, None]
        )
        amplitude = coupling / denominator
        square = amplitude * amplitude
        energy = -jnp.sum(square * denominator, axis=(2, 3)) / (virt_width * virt_width)
        kept = lax.reduce_precision(amplitude, exponent_bits=8, mantissa_bits=7)
        high = kept.astype(jnp.bfloat16)
        low = (amplitude - kept).astype(jnp.bfloat16)
        main = jnp.einsum("rtab,rtcb->ac", high, high, preferred_element_type=jnp.float32)
        side = jnp.einsum("rtab,rtcb->ac", high, low, preferred_element_type=jnp.float32)
        return main, side, energy

    def add(one, other):
        return tuple(a + b for a, b in zip(one, other))

    zero = add(
        tile(ints, ints, virt_own, occ_own, occ_own),
        tile(ints, mirror, virt_mirror, occ_own, occ_own),
    )
    one = None
    for piece, (near, far) in zip(back_pieces, virt_pieces):
        part = add(
            tile(ints, piece, near, occ_own, occ_back),
            tile(ints, from_partner(piece, "grp", 0), far, occ_own, occ_back),
        )
        one = part if one is None else add(one, part)
    further = jnp.concatenate(further_pieces, axis=1)
    two = add(
        tile(further, ints, virt_own, occ_further, occ_own),
        tile(further, mirror, virt_mirror, occ_further, occ_own),
    )
    three = None
    for piece, (near, far) in zip(back_pieces, virt_pieces):
        part = add(
            tile(further, piece, near, occ_further, occ_back),
            tile(further, from_partner(piece, "grp", 0), far, occ_further, occ_back),
        )
        three = part if three is None else add(three, part)
    main, side = add(add(zero[:2], one[:2]), add(two[:2], three[:2]))
    density = main + side + side.T
    shares = lax.psum_scatter(density, "blk", scatter_dimension=0, tiled=True) / (
        occ_count * STEPS * occ_dev
    )
    sent = shifted(jnp.concatenate([two[2], three[2]], axis=1), "blk", 2)
    energies = jnp.concatenate([zero[2], one[2], sent], axis=1)
    return (shares, energies + from_partner(energies, "grp", 0))


MESH = pl.DeviceIdType.MESH
TILE = 256
SLICE = 256
ROWS = 64
NT = (((1,), (1,)), ((), ()))


def product(rows, cols):
    return lax.dot_general(rows, cols, NT, preferred_element_type=jnp.float32)


def fused_kernel(
    count,
    ints_ref,
    energy_in,
    window_in,
    virt_in,
    density_ref,
    pairs_ref,
    energy_ref,
    window_ref,
    virt_ref,
    buf,
    mir,
    acc,
    dens,
    split,
    rows_virt,
    cols_virt,
    first_in,
    second_in,
    third_in,
    evec,
    ein,
    etot,
    eback,
    efar,
    efin,
    small_sem,
    load_sem,
    send_sem,
    recv_sem,
    mirror_send,
    mirror_recv,
    first_send,
    first_recv,
    second_send,
    second_recv,
    third_send,
    third_recv,
    energy_send,
    energy_recv,
):
    g = lax.axis_index("grp")
    me = lax.axis_index("blk")
    slices, width, depth = buf.shape[1:]
    layers = count // 4
    slab = dens.shape[3]
    tiles = width // TILE
    parts = width // 128
    place = me % 4
    x_at, y_at, z_at = me % 2, (me // 2) % 2, me // 4
    odd = place % 2
    even = odd == 0
    mirror = g + 1 - 2 * (g % 2)

    def at(offset):
        return (me + offset + count) % count

    x_peer = me + 1 - 2 * x_at
    y_peer = me + 2 - 4 * y_at
    is_two = (place // 2) * (1 - odd)
    col_to = at(1 - 2 * odd + 4 * (place // 3))
    other_to = at(2 - 4 * ((place + 3) // 4))
    other_slot = 2 + odd
    b_slot = 2 * (1 - odd)
    r_slot = 3 - 3 * is_two
    col_id = at(1 - 2 * ((place + 3) // 4) - 2 * is_two)
    b_id = at((1 - odd) * (2 - 4 * is_two))
    r_id = at(2 * odd + 4 * (1 - odd) * (1 - is_two))

    barrier = pltpu.get_barrier_semaphore()
    peers = [(g, x_peer), (mirror, me)]
    peers += [(g, at(o)) for o in (2, -2, 3, -3)]
    peers += [(g, at(4 * n)) for n in range(1, layers)]
    for peer in peers:
        pl.semaphore_signal(barrier, inc=1, device_id=peer, device_id_type=MESH)

    def load(k):
        return pltpu.make_async_copy(
            ints_ref.at[:, pl.ds(pl.multiple_of(k * depth, depth), depth)],
            buf.at[0, k],
            load_sem.at[k],
        )

    def flow(lane, k, slot, to):
        return pltpu.make_async_remote_copy(
            src_ref=buf.at[0, k],
            dst_ref=buf.at[slot, k],
            send_sem=send_sem.at[lane, k],
            recv_sem=recv_sem.at[lane, k],
            device_id=(g, to),
            device_id_type=MESH,
        )

    def flow_col(k):
        return flow(0, k, 1, col_to)

    def flow_other(k):
        return flow(1, k, other_slot, other_to)

    def flow_down(k):
        return flow(2, k, 3, at(-4))

    def reflect(slot, k):
        return pltpu.make_async_remote_copy(
            src_ref=buf.at[slot, k],
            dst_ref=mir.at[slot, k],
            send_sem=mirror_send.at[slot, k],
            recv_sem=mirror_recv.at[slot, k],
            device_id=(mirror, me),
            device_id_type=MESH,
        )

    small = [
        pltpu.make_async_copy(source, target, small_sem.at[n])
        for n, (source, target) in enumerate(
            ((energy_in, energy_ref), (window_in, window_ref), (virt_in, virt_ref))
        )
    ]

    @pl.loop(0, slices)
    def _(k):
        load(k).start()

    for copy in small:
        copy.start()

    pl.semaphore_wait(barrier, len(peers))

    @pl.loop(0, slices)
    def _(k):
        load(k).wait()
        flow_col(k).start()
        flow_other(k).start()

        @pl.when(place == 0)
        def _():
            flow_down(k).start()

        reflect(0, k).start()

    for copy in small:
        copy.wait()

    def virt_row(group, n):
        return virt_ref[pl.ds(group * parts + n, 1), :]

    for n in range(parts):
        mine, theirs = virt_row(g, n), virt_row(mirror, n)
        lanes = slice(n % 2 * 128, (n % 2 + 1) * 128)
        cols_virt[n // 2, :, lanes] = mine
        cols_virt[tiles + n // 2, :, lanes] = theirs
        rows_virt[n * 128 : (n + 1) * 128, :] = jnp.transpose(jnp.broadcast_to(mine, (128, 128)))

    def level(index):
        return energy_ref[window_ref[index]]

    own_level, col_level, b_level, r_level = level(me), level(col_id), level(b_id), level(r_id)

    def clear(pair):
        @pl.loop(0, 2 * tiles)
        def _(n):
            acc[pair, n] = jnp.zeros(acc.shape[2:], jnp.float32)

    def couple(pair, row_slot, k, cols, first_at):
        for n in range(tiles):
            side = cols[n * TILE : (n + 1) * TILE, :]
            for r in range(0, width, TILE):
                rows = slice(r, r + TILE)
                acc[pair, first_at + n, rows] += product(buf[row_slot, k, rows], side)

    def couple_near(pair, row_slot, col_slot, k):
        couple(pair, row_slot, k, buf.at[col_slot, k], 0)

    def couple_far(pair, row_slot, col_slot, k):
        couple(pair, row_slot, k, mir.at[col_slot, k], tiles)

    def amplitudes(pair, n, levels, energy_at, highs, lows):
        total = jnp.zeros((8, 128), jnp.float32)
        shifted_cols = [
            cols_virt[n, :, h * 128 : (h + 1) * 128] - levels for h in range(TILE // 128)
        ]
        for r in range(width // ROWS):
            span = slice(r * ROWS, (r + 1) * ROWS)
            base = rows_virt[span, :]
            for h in range(TILE // 128):
                lanes = slice(h * 128, (h + 1) * 128)
                coupling = acc[pair, n, span, lanes]
                amplitude = coupling / (base + shifted_cols[h])
                term = amplitude * coupling
                total = total + jnp.sum(term.reshape(ROWS // 8, 8, 128), axis=0)
                high = amplitude.astype(jnp.bfloat16)
                highs[span, lanes] = high
                lows[span, lanes] = (amplitude - high.astype(jnp.float32)).astype(jnp.bfloat16)
        evec[energy_at] += total

    def slabs_of(start, stop):
        for s in range(start // slab, -(-stop // slab)):
            low, high = max(start, s * slab), min(stop, (s + 1) * slab)
            yield (s // 4, (s // 2) % 2, s % 2), low, high, s * slab

    def densities(n, *splits, step=None):
        start, stop = n * TILE, (n + 1) * TILE
        step = step or TILE
        for first_row in range(0, stop, step):
            end_row = first_row + step
            update = None
            for highs, lows in splits:
                high, low = highs[first_row:end_row, :], lows[first_row:end_row, :]
                turn_high, turn_low = highs[start:stop, :], lows[start:stop, :]
                part = product(
                    jnp.concatenate([high, high, low], axis=1),
                    jnp.concatenate([turn_high, turn_low, turn_high], axis=1),
                )
                update = part if update is None else update + part
            for where, low_row, high_row, origin in slabs_of(first_row, end_row):
                dens[
                    (*where, slice(low_row - origin, high_row - origin), slice(start, stop))
                ] += update[low_row - first_row : high_row - first_row]

    evec[...] = jnp.zeros(evec.shape, jnp.float32)
    dens[...] = jnp.zeros(dens.shape, jnp.float32)

    clear(0)

    @pl.loop(0, slices)
    def _(k):
        couple_near(0, 0, 0, k)

    @pl.loop(0, slices)
    def _(k):
        reflect(0, k).wait_recv()
        couple_far(0, 0, 0, k)

    @pl.loop(0, 2 * tiles)
    def _(n):
        amplitudes(0, n, own_level + own_level, 0, split.at[0], split.at[1])
        for m in range(tiles):
            densities(m, (split.at[0], split.at[1]))

    for pair in range(3):
        clear(pair)

    @pl.loop(0, slices)
    def _(k):
        flow_col(k).wait_recv()
        reflect(1, k).start()
        flow_other(k).wait_recv()

        @pl.when(even)
        def _():
            reflect(2, k).start()

        @pl.when(place == 0)
        def _():
            flow_down(k).wait_recv()

        couple_near(0, b_slot, 1, k)
        couple_near(1, r_slot, b_slot, k)
        couple_near(2, r_slot, 1, k)
        reflect(1, k).wait_recv()

        @pl.when(even)
        def _():
            reflect(2, k).wait_recv()

        couple_far(0, b_slot, 1, k)
        couple_far(1, r_slot, b_slot, k)
        couple_far(2, r_slot, 1, k)

    @pl.loop(0, slices)
    def _(k):
        reflect(1, k).wait_send()

        @pl.when(even)
        def _():
            reflect(2, k).wait_send()

    def levels_of(pair):
        return jnp.where(
            pair == 0,
            b_level + col_level,
            jnp.where(pair == 1, r_level + b_level, r_level + col_level),
        )

    def kept(half, store):
        first_slot = store.shape[0] - 3
        slot, at_slice = half // (slices // 2), half % (slices // 2)
        return store.at[first_slot + slot, 2 * at_slice], store.at[first_slot + slot, 2 * at_slice + 1]

    def finish(t, highs, lows):
        pair, n = t // (2 * tiles), t % (2 * tiles)
        amplitudes(pair, n, levels_of(pair), 1 + pair, highs, lows)

    last = tiles - 1
    halves = 3 * tiles
    finish(0, *kept(0, mir))

    @pl.loop(0, halves - 1)
    def _(half):
        finish(2 * half + 1, *kept(half, buf))
        densities(last, kept(half, mir))
        finish(2 * half + 2, *kept(half + 1, mir))
        densities(last, kept(half, buf))

    finish(6 * tiles - 1, *kept(halves - 1, buf))
    densities(last, kept(halves - 1, mir))
    densities(last, kept(halves - 1, buf))

    def turn(n, m):
        block = [
            dens[(*where, slice(low - origin, high - origin), slice(m * TILE, (m + 1) * TILE))]
            for where, low, high, origin in slabs_of(n * TILE, (n + 1) * TILE)
        ]
        turned = jnp.transpose(jnp.concatenate(block, axis=0))
        for where, low, high, origin in slabs_of(m * TILE, (m + 1) * TILE):
            dens[(*where, slice(low - origin, high - origin), slice(n * TILE, (n + 1) * TILE))] = (
                turned[low - m * TILE : high - m * TILE]
            )

    def remote(source, target, sent, received, to):
        return pltpu.make_async_remote_copy(
            src_ref=source,
            dst_ref=target,
            send_sem=sent,
            recv_sem=received,
            device_id=to,
            device_id_type=MESH,
        )

    def lanes_of(n):
        return slice(n * 128, (n + 1) * 128)

    def first(n):
        if n % 2 == 0:
            source, to = dens.at[:, :, 1 - x_at, :, lanes_of(n)], x_peer
        else:
            source, to = dens.at[:, 1 - y_at, :, :, lanes_of(n)], y_peer
        return remote(source, first_in.at[n], first_send.at[n], first_recv.at[n], (g, to))

    def second(n):
        if n % 2 == 0:
            source, to = dens.at[:, 1 - y_at, x_at, :, lanes_of(n)], y_peer
        else:
            source, to = dens.at[:, y_at, 1 - x_at, :, lanes_of(n)], x_peer
        return remote(source, second_in.at[n], second_send.at[n], second_recv.at[n], (g, to))

    def third(n, step):
        to = at(4 * step)
        return remote(
            dens.at[to // 4, y_at, x_at, :, lanes_of(n)],
            third_in.at[n, step - 1],
            third_send.at[n, step - 1],
            third_recv.at[n, step - 1],
            (g, to),
        )

    for n in (2 * last, 2 * last + 1):
        first(n).start()

    share = remote(evec, ein, energy_send.at[0], energy_recv.at[0], (mirror, me))
    share.start()
    for m in range(last):
        turn(m, last)
    to_b = remote(etot.at[1], eback, energy_send.at[1], energy_recv.at[1], (g, y_peer))
    to_r = remote(etot.at[pl.ds(2, 2)], efar, energy_send.at[2], energy_recv.at[2], (g, r_id))

    def take_first(n):
        first(n).wait_recv()
        if n % 2 == 0:
            dens[:, :, x_at, :, lanes_of(n)] += first_in[n]
        else:
            dens[:, y_at, :, :, lanes_of(n)] += first_in[n]
        second(n).start()

    def take_second(n):
        second(n).wait_recv()
        dens[:, y_at, x_at, :, lanes_of(n)] += second_in[n]
        for step in range(1, layers):
            third(n, step).start()

    waiting = [2 * last, 2 * last + 1]
    halfway = []
    for n in range(last - 1, -1, -1):

        @pl.loop(0, 3)
        def _(third_of):
            densities(
                n,
                *(
                    kept(third_of * tiles + step, store)
                    for step in range(tiles)
                    for store in (mir, buf)
                ),
            )

        for m in (2 * n, 2 * n + 1):
            first(m).start()
        for m in range(n):
            turn(m, n)
        if n == last - 1:
            share.wait()
            etot[...] = evec[...] + ein[...]

            @pl.when(even)
            def _():
                to_b.start()

            @pl.when(is_two == 0)
            def _():
                to_r.start()

        for m in waiting:
            take_first(m)
        for m in halfway:
            take_second(m)
        waiting, halfway = [2 * n, 2 * n + 1], waiting
    for m in waiting:
        take_first(m)
    for m in halfway + waiting:
        take_second(m)

    @pl.loop(0, slices)
    def _(k):
        flow_col(k).wait_send()
        flow_other(k).wait_send()
        reflect(0, k).wait_send()

        @pl.when(place == 0)
        def _():
            flow_down(k).wait_send()

    efin[...] = etot[...]

    @pl.when(even)
    def _():
        to_b.wait()
        efin[1] = eback[...]

    @pl.when(is_two == 0)
    def _():
        to_r.wait()
        efin[2:4] = efar[...]

    lane = lax.broadcasted_iota(jnp.int32, (1, 4), 1)
    energies = jnp.zeros((1, 4), jnp.float32)
    for s in range(4):
        energies = jnp.where(lane == s, -jnp.sum(efin[s]) / (width * width), energies)
    pairs_ref[...] = energies

    for n in sorted(range(parts), key=lambda piece: -(piece // 2)):
        value = dens[z_at, y_at, x_at, :, lanes_of(n)]
        for step in range(1, layers):
            third(n, step).wait_recv()
            value = value + third_in[n, step - 1]
        density_ref[:, lanes_of(n)] = value / (count * STEPS)

    for n in range(parts):
        first(n).wait_send()
        second(n).wait_send()
        for step in range(1, layers):
            third(n, step).wait_send()


def fused(count, ints, occ_energy, occ_window, virt_energy):
    width, depth = ints.shape[1:]
    slices, layers, slab = depth // SLICE, count // 4, width // count
    tiles, parts = width // TILE, width // 128
    dma = pltpu.SemaphoreType.DMA
    return pl.pallas_call(
        functools.partial(fused_kernel, count),
        out_shape=(
            jax.ShapeDtypeStruct((slab, width), jnp.float32),
            jax.ShapeDtypeStruct((1, STEPS), jnp.float32),
        ),
        in_specs=[
            pl.BlockSpec(memory_space=pl.ANY),
            pl.BlockSpec(memory_space=pl.ANY),
            pl.BlockSpec(memory_space=pl.ANY),
            pl.BlockSpec(memory_space=pl.ANY),
        ],
        out_specs=(
            pl.BlockSpec(memory_space=pltpu.VMEM),
            pl.BlockSpec(memory_space=pltpu.VMEM),
        ),
        scratch_shapes=[
            pltpu.SMEM(occ_energy.shape, jnp.float32),
            pltpu.SMEM(occ_window.shape, jnp.int32),
            pltpu.VMEM((virt_energy.shape[0] // 128, 128), jnp.float32),
            pltpu.VMEM((4, slices, width, SLICE), jnp.bfloat16),
            pltpu.VMEM((3, slices, width, SLICE), jnp.bfloat16),
            pltpu.VMEM((3, 2 * tiles, width, TILE), jnp.float32),
            pltpu.VMEM((layers, 2, 2, slab, width), jnp.float32),
            pltpu.VMEM((2, width, TILE), jnp.bfloat16),
            pltpu.VMEM((width, 128), jnp.float32),
            pltpu.VMEM((2 * tiles, 1, TILE), jnp.float32),
            pltpu.VMEM((parts, layers, 2, slab, 128), jnp.float32),
            pltpu.VMEM((parts, layers, slab, 128), jnp.float32),
            pltpu.VMEM((parts, layers - 1, slab, 128), jnp.float32),
            pltpu.VMEM((4, 8, 128), jnp.float32),
            pltpu.VMEM((4, 8, 128), jnp.float32),
            pltpu.VMEM((4, 8, 128), jnp.float32),
            pltpu.VMEM((8, 128), jnp.float32),
            pltpu.VMEM((2, 8, 128), jnp.float32),
            pltpu.VMEM((4, 8, 128), jnp.float32),
            dma((3,)),
            dma((slices,)),
            dma((3, slices)),
            dma((3, slices)),
            dma((3, slices)),
            dma((3, slices)),
            dma((parts,)),
            dma((parts,)),
            dma((parts,)),
            dma((parts,)),
            dma((parts, layers - 1)),
            dma((parts, layers - 1)),
            dma((3,)),
            dma((3,)),
        ],
        compiler_params=pltpu.CompilerParams(
            collective_id=0, has_side_effects=True, vmem_limit_bytes=67043328
        ),
    )(ints[0], occ_energy, occ_window, virt_energy.reshape(-1, 128))


def fused_or_local(mesh, ints, occ_energy, occ_window, virt_energy):
    groups, blocks = mesh.shape["grp"], mesh.shape["blk"]
    occ_dev, width, depth = ints.shape
    fits = occ_dev == 1 and STEPS == 4 and groups % 2 == 0 and blocks % 4 == 0 and blocks >= 8
    fits = fits and width % TILE == 0 and width % (8 * blocks) == 0 and depth % SLICE == 0
    fits = fits and width > TILE and depth // SLICE >= 4 * (width // TILE)
    if fits:
        return fused(blocks, ints, occ_energy, occ_window, virt_energy)
    return local(ints, occ_energy, occ_window, virt_energy)


def solution(mesh):
    return jax.shard_map(
        functools.partial(fused_or_local, mesh),
        mesh=mesh,
        in_specs=(P("blk", "grp", None), P(), P(), P()),
        out_specs=(P(("grp", "blk"), None), P("blk", None)),
        check_vma=False,
    )
```
